32 devices in a mesh: section: 4 (over y, core), row: 4 (over z), col: 2 (over x).
Axes of the slice: x: 2, y: 2, z: 4, core: 2. Of those that a mesh axis runs over, the one named last changes fastest.
Arguments:
- section_input: bfloat16 [4, 2, 32, 32, 128], P('section', None, 'row', 'col'), may hold values from -6 to 6
- first_pre: bfloat16 [4, 2, 32, 32, 128], P('section', None, 'row', 'col'), may hold values from -6 to 6
- second_pre: bfloat16 [4, 2, 32, 32, 128], P('section', None, 'row', 'col'), may hold values from -6 to 6
- out_grad: bfloat16 [2, 32, 32, 128], P(None, 'row', 'col'), may hold values from -6 to 6
- kernels: bfloat16 [4, 2, 3, 3, 128, 128], P('section'), may hold values from -0.1875 to 0.1875
- bn_scale: float32 [4, 2, 128], P('section'), may hold values from 0.5 to 2
- bn_shift: float32 [4, 2, 128], P('section'), may hold values from -3 to 3
Outputs:
- input_grad: bfloat16 [4, 2, 32, 32, 128], P('section', None, 'row', 'col')
- filter_grad: float32 [4, 2, 3, 3, 128, 128], P('section')
The draws below stay inside these ranges and needn't reach their ends.
All inputs are finite; a program needn't handle non-finite values.
Results may differ from the reference program's by a relative error of at most 0.013.
Values may be sent and summed in bfloat16 or wider, within the bound.
A program may use at most 64 MiB of HBM per device.

```python
import math
import jax
import jax.numpy as jnp
from jax import lax

CHANNELS = 128
MICRO = 2
SECTIONS = 4
IMG_ROWS = 32
IMG_COLS = 32


def shard_levels(own_key, extent, shards, smallest, high):
    def one(dim, shards_of):
        steps = jax.random.uniform(jax.random.fold_in(jax.random.fold_in(own_key, 6), dim), (shards_of,), jnp.float32, smallest / len(shards), high / len(shards))
        return jnp.repeat(jnp.exp(steps), extent[dim] // shards_of).reshape((-1,) + (1,) * (len(extent) - dim - 1))

    factor_of = one(*shards[0])
    for cut in shards[1:]:
        factor_of = factor_of * one(*cut)
    return factor_of


def normal_values(key, dims, scale, bound, cuts=(), dtype=jnp.bfloat16):
    drawn = jax.random.normal(key, dims, jnp.float32) * scale
    if len(cuts) > 0:
        drawn = shard_levels(key, dims, cuts, -0.22, 0.18) * drawn
    return jnp.clip(drawn, min=-bound, max=bound).astype(dtype)


def setup_inputs(seed: int = 0) -> dict:
    arg_keys = jax.random.split(jax.random.key(seed), 8)
    return {
        "section_input": normal_values(arg_keys[0], (SECTIONS, MICRO, IMG_ROWS, IMG_COLS, CHANNELS), 1.0, 6.0, ((0, 4), (2, 4), (3, 2))),
        "first_pre": normal_values(arg_keys[1], (SECTIONS, MICRO, IMG_ROWS, IMG_COLS, CHANNELS), 1.0, 6.0, ((0, 4), (2, 4), (3, 2))),
        "second_pre": normal_values(arg_keys[2], (SECTIONS, MICRO, IMG_ROWS, IMG_COLS, CHANNELS), 1.0, 6.0, ((0, 4), (2, 4), (3, 2))),
        "out_grad": normal_values(arg_keys[3], (MICRO, IMG_ROWS, IMG_COLS, CHANNELS), 1.0, 6.0, ((1, 4), (2, 2))),
        "kernels": normal_values(arg_keys[4], (SECTIONS, 2, 3, 3, CHANNELS, CHANNELS), (9 * CHANNELS) ** -0.5, 0.1875, ((0, 4),)),
        "bn_scale": jnp.clip(jnp.exp(math.log(2.0) - 1.3862944 * jax.random.uniform(arg_keys[5], (SECTIONS, 2, CHANNELS), jnp.float32) ** shard_levels(arg_keys[5], (SECTIONS, 2, CHANNELS), ((0, 4),), -0.2, 0.2)), 0.5, 2.0),
        "bn_shift": normal_values(arg_keys[6], (SECTIONS, 2, CHANNELS), 0.5, 3.0, ((0, 4),), jnp.float32),
    }


def padded_tile(field):
    return jnp.pad(field, ((1, 1), (1, 1), (0, 0)))

def correlate(padded, kernel):
    result = lax.conv_general_dilated(padded[None], kernel, (1, 1), 'VALID', dimension_numbers=('NHWC', 'HWIO', 'NHWC'), preferred_element_type=jnp.float32)
    return result[0]

def flip_kernel(kernel):
    return jnp.transpose(jnp.flip(kernel, (0, 1)), (0, 1, 3, 2))

def kernel_grad(padded, gradient):
    rows_here, cols_here = (gradient.shape[0], gradient.shape[1])
    pieces = []
    for row_off in range(3):
        for col_off in range(3):
            window = padded[row_off:row_off + rows_here, col_off:col_off + cols_here]
            pieces.append(jnp.einsum('hwc,hwd->cd', window, gradient, preferred_element_type=jnp.float32))
    return jnp.stack(pieces).reshape(3, 3, gradient.shape[2], gradient.shape[2])

def unit_backward(inputs, first_pre, second_pre, incoming, kernel, scales, shifts):
    first_norm = scales[0] * first_pre.astype(jnp.float32) + shifts[0]
    first_act = jnp.maximum(first_norm, 0.0).astype(jnp.bfloat16)
    second_norm = scales[1] * second_pre.astype(jnp.float32) + shifts[1]
    masked = jnp.where(second_norm + inputs.astype(jnp.float32) > 0, incoming.astype(jnp.float32), 0.0)
    second_grad = (scales[1] * masked).astype(jnp.bfloat16)
    act_grad = correlate(padded_tile(second_grad), flip_kernel(kernel[1]))
    first_grad = (scales[0] * jnp.where(first_norm > 0, act_grad, 0.0)).astype(jnp.bfloat16)
    input_grad = (masked + correlate(padded_tile(first_grad), flip_kernel(kernel[0]))).astype(jnp.bfloat16)
    grads = jnp.stack([kernel_grad(padded_tile(inputs), first_grad), kernel_grad(padded_tile(first_act), second_grad)])
    return (input_grad, grads)

def reference(section_input, first_pre, second_pre, out_grad, kernels, bn_scale, bn_shift):
    outputs = [[None] * MICRO for _ in range(SECTIONS)]
    filters = [jnp.zeros((2, 3, 3, CHANNELS, CHANNELS), jnp.float32) for _ in range(SECTIONS)]
    for micro_index in range(MICRO):
        incoming = out_grad[micro_index]
        for section_index in reversed(range(SECTIONS)):
            incoming, grads = unit_backward(section_input[section_index, micro_index], first_pre[section_index, micro_index], second_pre[section_index, micro_index], incoming, kernels[section_index], bn_scale[section_index], bn_shift[section_index])
            outputs[section_index][micro_index] = incoming
            filters[section_index] = filters[section_index] + grads
    factor = 1.0 / jnp.sqrt(jnp.float32(MICRO * IMG_ROWS * IMG_COLS))
    input_grad = jnp.stack([jnp.stack(column) for column in outputs])
    filter_grad = jnp.stack(filters) * factor
    return (input_grad, filter_grad)
```

```python
import functools

import jax
import jax.numpy as jnp
from jax import lax
from jax.experimental import pallas as pl
from jax.experimental.pallas import tpu as pltpu
from jax.sharding import PartitionSpec as P

MESH = pl.DeviceIdType.MESH
SPREAD = [(dr, dc) for dr in (-1, 0, 1) for dc in (-1, 0, 1)]
F32 = jnp.float32
BF16 = jnp.bfloat16


def each(count, body):
    if count <= 16:
        for step in range(count):
            body(step)
    else:

        def run(step, carry):
            body(step)
            return carry

        lax.fori_loop(0, count, run, 0)


def kernel(
    dims, x_ref, p1_ref, p2_ref, og_ref, k_ref, scale_ref, shift_ref,
    out_ref, fg_ref,
    xf, p1f, p2f, gf, kt, c1, c2, cols1, cols2, act, red, inbox, final, gathered,
    halo_send, halo_recv, og_send, g_send, g_recv, rs_send, rs_recv, ag_send, ag_recv,
):
    axes, sections, rows_n, cols_n, factor = dims
    micros, rows, cols, width = x_ref.shape
    pitch = 2 * cols
    half = cols // 2
    group = rows_n * cols_n
    chunk = final.shape[0]
    s = lax.axis_index("section")
    r = lax.axis_index("row")
    c = lax.axis_index("col")
    me = r * cols_n + c

    def dev(sec, row, col):
        where = {"section": sec, "row": row, "col": col}
        return tuple(where[a] for a in axes)

    def inside(dr, dc):
        return (r + dr >= 0) & (r + dr < rows_n) & (c + dc >= 0) & (c + dc < cols_n)

    def src_part(dr, dc):
        row = {-1: pl.ds(0, 2), 0: pl.ds(0, rows), 1: pl.ds(rows - 2, 2)}[dr]
        col = {-1: pl.ds(0, half), 0: pl.ds(0, cols), 1: pl.ds(half, half)}[dc]
        return row, col

    def dst_part(dr, dc):
        row = {-1: pl.ds(rows + 2, 2), 0: pl.ds(2, rows), 1: pl.ds(0, 2)}[dr]
        col = {-1: pl.ds(cols, half), 0: pl.ds(0, cols), 1: pl.ds(cols + half, half)}[dc]
        return row, col

    def shift_copy(src, dst, m, dr, dc, send, recv, sec):
        a, b = src_part(dr, dc)
        p, q = dst_part(dr, dc)
        return pltpu.make_async_remote_copy(
            src_ref=src.at[m, a, b], dst_ref=dst.at[m, p, q],
            send_sem=send, recv_sem=recv,
            device_id=dev(sec, r + dr, c + dc), device_id_type=MESH,
        )

    for ref in (xf, p1f, p2f, gf):
        ref[...] = jnp.zeros(ref.shape, ref.dtype)

    barrier = pltpu.get_barrier_semaphore()

    def greet(step):
        peer = lax.rem(me + step + 1, group)
        pl.semaphore_signal(
            barrier, inc=1, device_id=dev(s, peer // cols_n, lax.rem(peer, cols_n)),
            device_id_type=MESH,
        )

    each(group - 1, greet)
    expected = group - 1 + jnp.int32(0)
    for dr, dc in SPREAD:
        expected = expected + jnp.where((s > 0) & inside(dr, dc), 1, 0)

        @pl.when((s < sections - 1) & inside(dr, dc))
        def _():
            pl.semaphore_signal(
                barrier, inc=1, device_id=dev(s + 1, r + dr, c + dc), device_id_type=MESH
            )

    pl.semaphore_wait(barrier, expected)

    halos = ((p2_ref, p2f), (x_ref, xf), (p1_ref, p1f))
    around = [(d, dr, dc) for d, (dr, dc) in enumerate(SPREAD) if (dr, dc) != (0, 0)]

    def halo_copy(m, which, d, dr, dc):
        src, dst = halos[which]
        return shift_copy(
            src, dst, m, dr, dc, halo_send.at[m, which, d], halo_recv.at[m, which, d], s
        )

    def out_grad_copy(m, d, dr, dc):
        return shift_copy(og_ref, gf, m, dr, dc, og_send.at[m, d], g_recv.at[m, d], s)

    def section_copy(m, d, dr, dc):
        return shift_copy(
            out_ref, gf, m, dr, dc, g_send.at[m, d], g_recv.at[m, d], s - 1
        )

    for m in range(micros):
        for d, dr, dc in around:

            @pl.when(inside(dr, dc) & (s == sections - 1))
            def _():
                out_grad_copy(m, d, dr, dc).start()

            @pl.when(inside(dr, dc))
            def _():
                for which in range(3):
                    halo_copy(m, which, d, dr, dc).start()

    for conv in range(2):
        for k in range(9):
            kt[conv, pl.ds(k * width, width), :] = jnp.transpose(k_ref[conv, 8 - k])

    for src, dst in halos:
        dst[:, pl.ds(2, rows), pl.ds(0, cols), :] = src[...]

    @pl.when(s == sections - 1)
    def _():
        gf[:, pl.ds(2, rows), pl.ds(0, cols), :] = og_ref[...]

    g0 = scale_ref[0:1, :].reshape(1, 1, width)
    g1 = scale_ref[1:2, :].reshape(1, 1, width)
    b0 = shift_ref[0:1, :].reshape(1, 1, width)
    b1 = shift_ref[1:2, :].reshape(1, 1, width)
    for m in range(micros):
        first_norm = g0 * p1_ref[m].astype(F32) + b0
        act[pl.ds(m * rows * cols, rows * cols), :] = (
            jnp.maximum(first_norm, 0.0).astype(BF16).reshape(rows * cols, width)
        )

    row_i = lax.broadcasted_iota(jnp.int32, (rows + 2, pitch, width), 0)
    col_i = lax.broadcasted_iota(jnp.int32, (rows + 2, pitch, width), 1)
    row_lo = jnp.where(r == 0, 1, 0)
    row_hi = jnp.where(r == rows_n - 1, rows, rows + 1)
    col_hi = jnp.where(c == cols_n - 1, cols, cols + half)
    col_lo = jnp.where(c == 0, pitch, cols + half)
    valid = (
        (row_i >= row_lo) & (row_i <= row_hi) & ((col_i < col_hi) | (col_i >= col_lo))
    )

    def wrapped(field):
        left = pltpu.roll(field, 1, 1)
        right = pltpu.roll(field, pitch - 1, 1)
        return left.astype(BF16), field.astype(BF16), right.astype(BF16)

    for m in range(micros):
        for d, dr, dc in around:

            @pl.when(inside(-dr, -dc))
            def _():
                for which in range(3):
                    halo_copy(m, which, d, dr, dc).wait_recv()

        second_norm = g1 * p2f[m].astype(F32) + b1
        c2[...] = jnp.where(second_norm + xf[m].astype(F32) > 0, g1, 0.0)
        first_norm = g0 * p1f[m, pl.ds(1, rows + 2)].astype(F32) + b0
        c1[...] = jnp.where((first_norm > 0) & valid, g0, 0.0)

        for d, (dr, dc) in enumerate(SPREAD):
            if (dr, dc) == (0, 0):

                @pl.when(s < sections - 1)
                def _():
                    section_copy(m, d, dr, dc).wait_recv()
            else:

                @pl.when(inside(-dr, -dc))
                def _():
                    section_copy(m, d, dr, dc).wait_recv()

        incoming = gf[m].astype(F32)
        second_grad = (incoming * c2[...]).astype(BF16).astype(F32)
        acc = None
        moved = wrapped(second_grad)
        base = m * rows * cols
        for i in range(3):
            for j in range(3):
                k = 3 * i + j
                part = moved[j][i : i + rows + 2]
                cols2[pl.ds(base, rows * cols), pl.ds(k * width, width)] = part[
                    1 : rows + 1, :cols
                ].reshape(rows * cols, width)
                term = jnp.dot(
                    part.reshape((rows + 2) * pitch, width),
                    kt[1, pl.ds(k * width, width), :],
                    preferred_element_type=F32,
                )
                acc = term if acc is None else acc + term
        first_grad = (acc.reshape(rows + 2, pitch, width) * c1[...]).astype(BF16).astype(F32)
        moved = wrapped(first_grad)
        for i in range(3):
            for j in range(3):
                k = 3 * i + j
                cols1[pl.ds(base, rows * cols), pl.ds(k * width, width)] = moved[j][
                    i : i + rows, :cols
                ].reshape(rows * cols, width)
        back = jnp.dot(
            cols1[pl.ds(base, rows * cols), :], kt[0], preferred_element_type=F32
        )
        tile = (pl.ds(2, rows), pl.ds(0, cols))
        masked = jnp.where(c2[tile] > 0, gf[(m, *tile)].astype(F32), 0.0)
        out_ref[m] = (masked + back.reshape(rows, cols, width)).astype(BF16)
        for d, (dr, dc) in enumerate(SPREAD):

            @pl.when((s > 0) & inside(dr, dc))
            def _():
                section_copy(m, d, dr, dc).start()

    if red.shape[0] > 18 * width:
        red[pl.ds(18 * width, red.shape[0] - 18 * width), :] = jnp.zeros(
            (red.shape[0] - 18 * width, width), BF16
        )
    pixels = micros * rows * cols
    contract = (((0,), (0,)), ((), ()))
    fields = (x_ref[...].reshape(pixels, width), act[...])
    for conv, grads in ((1, cols2), (0, cols1)):
        total = lax.dot_general(fields[conv], grads[...], contract, preferred_element_type=F32)
        for k in range(9):
            red[pl.ds((conv * 9 + 8 - k) * width, width), :] = (
                total[:, k * width : (k + 1) * width] * factor
            ).astype(BF16)

    def piece(index):
        return pl.ds(pl.multiple_of(index * chunk, 16), chunk)

    def peer_of(step):
        peer = lax.rem(me + step + 1, group)
        return peer, dev(s, peer // cols_n, lax.rem(peer, cols_n))

    def rs_copy(step):
        peer, where = peer_of(step)
        return pltpu.make_async_remote_copy(
            src_ref=red.at[piece(peer)], dst_ref=inbox.at[step],
            send_sem=rs_send.at[step], recv_sem=rs_recv.at[step],
            device_id=where, device_id_type=MESH,
        )

    def ag_copy(step):
        peer, where = peer_of(step)
        return pltpu.make_async_remote_copy(
            src_ref=final, dst_ref=gathered.at[step],
            send_sem=ag_send.at[step], recv_sem=ag_recv.at[step],
            device_id=where, device_id_type=MESH,
        )

    each(group - 1, lambda step: rs_copy(step).start())
    fg_ref[piece(me), :] = red[piece(me), :].astype(F32)

    def gather_in(step):
        rs_copy(step).wait_recv()
        fg_ref[piece(me), :] += inbox[step].astype(F32)

    each(group - 1, gather_in)
    final[...] = fg_ref[piece(me), :].astype(BF16)
    each(group - 1, lambda step: ag_copy(step).start())

    def spread_out(step):
        ag_copy(step).wait_recv()
        source = lax.rem(me + group - step - 1, group)
        fg_ref[piece(source), :] = gathered[step].astype(F32)

    each(group - 1, spread_out)

    each(group - 1, lambda step: rs_copy(step).wait_send())
    each(group - 1, lambda step: ag_copy(step).wait_send())
    for m in range(micros):
        for d, (dr, dc) in enumerate(SPREAD):
            if (dr, dc) != (0, 0):

                @pl.when(inside(dr, dc))
                def _():
                    for which in range(3):
                        halo_copy(m, which, d, dr, dc).wait_send()

                @pl.when(inside(dr, dc) & (s == sections - 1))
                def _():
                    out_grad_copy(m, d, dr, dc).wait_send()

            @pl.when((s > 0) & inside(dr, dc))
            def _():
                section_copy(m, d, dr, dc).wait_send()


def on_device(axes, sizes, section_input, first_pre, second_pre, out_grad, kernels, bn_scale, bn_shift):
    sections, rows_n, cols_n = sizes
    micros, rows, cols, width = out_grad.shape
    group = rows_n * cols_n
    tiles = 18 * width // 16
    chunk = 16 * (-(-tiles // group))
    pixels = micros * rows * cols
    factor = 1.0 / (pixels * group) ** 0.5
    dims = (axes, sections, rows_n, cols_n, factor)
    pitch = 2 * cols
    dma = pltpu.SemaphoreType.DMA
    vmem = pl.BlockSpec(memory_space=pltpu.VMEM)
    field = pltpu.VMEM((micros, rows + 4, pitch, width), BF16)
    peers = max(group - 1, 1)
    out, grads = pl.pallas_call(
        functools.partial(kernel, dims),
        out_shape=(
            jax.ShapeDtypeStruct(out_grad.shape, BF16),
            jax.ShapeDtypeStruct((group * chunk, width), F32),
        ),
        in_specs=[vmem] * 7,
        out_specs=(vmem, vmem),
        scratch_shapes=[
            field, field, field, field,
            pltpu.VMEM((2, 9 * width, width), BF16),
            pltpu.VMEM((rows + 2, pitch, width), F32),
            pltpu.VMEM((rows + 4, pitch, width), F32),
            pltpu.VMEM((pixels, 9 * width), BF16),
            pltpu.VMEM((pixels, 9 * width), BF16),
            pltpu.VMEM((pixels, width), BF16),
            pltpu.VMEM((group * chunk, width), BF16),
            pltpu.VMEM((peers, chunk, width), BF16),
            pltpu.VMEM((chunk, width), BF16),
            pltpu.VMEM((peers, chunk, width), BF16),
            dma((micros, 3, 9)), dma((micros, 3, 9)),
            dma((micros, 9)), dma((micros, 9)), dma((micros, 9)),
            dma((peers,)), dma((peers,)), dma((peers,)), dma((peers,)),
        ],
        compiler_params=pltpu.CompilerParams(
            collective_id=0, has_side_effects=True, vmem_limit_bytes=48 * 1024 * 1024
        ),
    )(
        section_input[0], first_pre[0], second_pre[0], out_grad,
        kernels[0].reshape(2, 9, width, width), bn_scale[0], bn_shift[0],
    )
    grads = grads[: 18 * width].reshape(1, 2, 3, 3, width, width)
    return out[None], grads


def solution(mesh):
    in_specs = (
        P("section", None, "row", "col", None),
        P("section", None, "row", "col", None),
        P("section", None, "row", "col", None),
        P(None, "row", "col", None),
        P("section", None, None, None, None, None),
        P("section", None, None),
        P("section", None, None),
    )
    out_specs = (P("section", None, "row", "col", None), P("section", None, None, None, None, None))
    sizes = tuple(mesh.shape[a] for a in ("section", "row", "col"))
    return jax.shard_map(
        functools.partial(on_device, tuple(mesh.axis_names), sizes),
        mesh=mesh, in_specs=in_specs, out_specs=out_specs, check_vma=False,
    )
```

```python
import functools

import jax
import jax.numpy as jnp
from jax import lax
from jax.experimental import pallas as pl
from jax.experimental.pallas import tpu as pltpu
from jax.sharding import PartitionSpec as P

MESH = pl.DeviceIdType.MESH
SPREAD = [(dr, dc) for dr in (-1, 0, 1) for dc in (-1, 0, 1)]
F32 = jnp.float32
BF16 = jnp.bfloat16


def each(count, body):
    if count <= 16:
        for step in range(count):
            body(step)
    else:

        def run(step, carry):
            body(step)
            return carry

        lax.fori_loop(0, count, run, 0)


def kernel(
    dims, x_ref, p1_ref, p2_ref, og_ref, k_hbm, scale_hbm, shift_hbm,
    out_ref, fg_ref,
    xf, p1f, p2f, gf, k_ref, scale_ref, shift_ref, kt, c1, c2, cols1, cols2, act,
    union_x, union_g, spare_x, spare_g, crossed, red, inbox, final, gathered,
    local, pair_send, pair_recv, halo_send, halo_recv, og_send, g_send, g_recv, rs_send, rs_recv, ag_send, ag_recv,
):
    axes, sections, rows_n, cols_n, factor, paired = dims
    micros, rows, cols, width = x_ref.shape
    pitch = 2 * cols
    half = cols // 2
    group = rows_n * cols_n
    chunk = final.shape[0]
    s = lax.axis_index("section")
    r = lax.axis_index("row")
    c = lax.axis_index("col")
    me = r * cols_n + c

    def dev(sec, row, col):
        where = {"section": sec, "row": row, "col": col}
        return tuple(where[a] for a in axes)

    def inside(dr, dc):
        return (r + dr >= 0) & (r + dr < rows_n) & (c + dc >= 0) & (c + dc < cols_n)

    def src_part(dr, dc):
        row = {-1: pl.ds(0, 2), 0: pl.ds(0, rows), 1: pl.ds(rows - 2, 2)}[dr]
        col = {-1: pl.ds(0, half), 0: pl.ds(0, cols), 1: pl.ds(half, half)}[dc]
        return row, col

    def dst_part(dr, dc):
        row = {-1: pl.ds(rows + 2, 2), 0: pl.ds(2, rows), 1: pl.ds(0, 2)}[dr]
        col = {-1: pl.ds(cols, half), 0: pl.ds(0, cols), 1: pl.ds(cols + half, half)}[dc]
        return row, col

    def shift_copy(src, dst, m, dr, dc, send, recv, sec):
        a, b = src_part(dr, dc)
        p, q = dst_part(dr, dc)
        if src is dst:
            a = pl.ds(a.start + 2, a.size)
        return pltpu.make_async_remote_copy(
            src_ref=src.at[m, a, b], dst_ref=dst.at[m, p, q],
            send_sem=send, recv_sem=recv,
            device_id=dev(sec, r + dr, c + dc), device_id_type=MESH,
        )

    def centre(ref):
        return ref.at[:, pl.ds(2, rows), pl.ds(0, cols)]

    loads = [
        pltpu.make_async_copy(src, dst, local.at[i])
        for i, (src, dst) in enumerate(
            (
                (p2_ref, centre(p2f)), (x_ref, centre(xf)), (p1_ref, centre(p1f)),
                (scale_hbm, scale_ref), (shift_hbm, shift_ref), (k_hbm, k_ref),
            )
        )
    ]
    og_load = pltpu.make_async_copy(og_ref, centre(gf), local.at[6])

    @pl.when(s == sections - 1)
    def _():
        og_load.start()

    for load in loads:
        load.start()

    for ref in (xf, p1f, p2f, gf):
        for m in range(micros):
            ref[m, 0:2] = jnp.zeros((2, pitch, width), BF16)
            ref[m, rows + 2 : rows + 4] = jnp.zeros((2, pitch, width), BF16)
            ref[m, 2 : rows + 2, cols:pitch] = jnp.zeros((rows, cols, width), BF16)

    barrier = pltpu.get_barrier_semaphore()

    def greet(step):
        peer = lax.rem(me + step + 1, group)
        pl.semaphore_signal(
            barrier, inc=1, device_id=dev(s, peer // cols_n, lax.rem(peer, cols_n)),
            device_id_type=MESH,
        )

    each(group - 1, greet)
    expected = group - 1 + jnp.int32(0)
    for dr, dc in SPREAD:
        expected = expected + jnp.where((s > 0) & inside(dr, dc), 1, 0)

        @pl.when((s < sections - 1) & inside(dr, dc))
        def _():
            pl.semaphore_signal(
                barrier, inc=1, device_id=dev(s + 1, r + dr, c + dc), device_id_type=MESH
            )

    for load in loads[:3]:
        load.wait()

    @pl.when(s == sections - 1)
    def _():
        og_load.wait()

    pl.semaphore_wait(barrier, expected)

    halos = ((p2f, p2f), (xf, xf), (p1f, p1f))
    around = [(d, dr, dc) for d, (dr, dc) in enumerate(SPREAD) if (dr, dc) != (0, 0)]

    def halo_copy(m, which, d, dr, dc):
        src, dst = halos[which]
        return shift_copy(
            src, dst, m, dr, dc, halo_send.at[m, which, d], halo_recv.at[m, which, d], s
        )

    def out_grad_copy(m, d, dr, dc):
        return shift_copy(gf, gf, m, dr, dc, og_send.at[m, d], g_recv.at[m, d], s)

    def section_copy(m, d, dr, dc):
        return shift_copy(
            out_ref, gf, m, dr, dc, g_send.at[m, d], g_recv.at[m, d], s - 1
        )

    for m in range(micros):
        for d, dr, dc in around:

            @pl.when(inside(dr, dc) & (s == sections - 1))
            def _():
                out_grad_copy(m, d, dr, dc).start()

            @pl.when(inside(dr, dc))
            def _():
                for which in range(3):
                    halo_copy(m, which, d, dr, dc).start()

    for load in loads[3:]:
        load.wait()
    for conv in range(2):
        for k in range(9):
            kt[conv, pl.ds(k * width, width), :] = jnp.transpose(k_ref[conv, 8 - k])

    g0 = scale_ref[0:1, :].reshape(1, 1, width)
    g1 = scale_ref[1:2, :].reshape(1, 1, width)
    b0 = shift_ref[0:1, :].reshape(1, 1, width)
    b1 = shift_ref[1:2, :].reshape(1, 1, width)
    own = pl.ds(pl.multiple_of(c * cols, cols), cols)

    def pair_copy(m, which, src, dst):
        return pltpu.make_async_remote_copy(
            src_ref=src.at[m], dst_ref=dst.at[m, :, own],
            send_sem=pair_send.at[m, which], recv_sem=pair_recv.at[m, which],
            device_id=dev(s, r, 1 - c), device_id_type=MESH,
        )

    def pair_arrival(m, which, src, dst):
        other = pl.ds(pl.multiple_of((1 - c) * cols, cols), cols)
        return pltpu.make_async_remote_copy(
            src_ref=src.at[m], dst_ref=dst.at[m, :, other],
            send_sem=pair_send.at[m, which], recv_sem=pair_recv.at[m, which],
            device_id=dev(s, r, 1 - c), device_id_type=MESH,
        )

    pairs = ((spare_x, union_x), (spare_g, union_g))
    for m in range(micros):
        first_norm = g0 * p1f[m, 2 : rows + 2, :cols].astype(F32) + b0
        active = jnp.maximum(first_norm, 0.0)
        if paired:
            inputs = xf[m, 2 : rows + 2, :cols].astype(F32)
            union_x[m, :, own] = jnp.where(c == 0, inputs, active).astype(BF16)
            spare_x[m] = jnp.where(c == 0, active, inputs).astype(BF16)
            pair_copy(m, 0, *pairs[0]).start()
        else:
            act[pl.ds(m * rows * cols, rows * cols), :] = active.astype(BF16).reshape(
                rows * cols, width
            )

    row_i = lax.broadcasted_iota(jnp.int32, (rows + 2, pitch, width), 0)
    col_i = lax.broadcasted_iota(jnp.int32, (rows + 2, pitch, width), 1)
    row_lo = jnp.where(r == 0, 1, 0)
    row_hi = jnp.where(r == rows_n - 1, rows, rows + 1)
    col_hi = jnp.where(c == cols_n - 1, cols, cols + half)
    col_lo = jnp.where(c == 0, pitch, cols + half)
    valid = (
        (row_i >= row_lo) & (row_i <= row_hi) & ((col_i < col_hi) | (col_i >= col_lo))
    )

    def wrapped(field):
        left = pltpu.roll(field, 1, 1)
        right = pltpu.roll(field, pitch - 1, 1)
        return left.astype(BF16), field.astype(BF16), right.astype(BF16)

    for m in range(micros):
        for d, dr, dc in around:

            @pl.when(inside(-dr, -dc))
            def _():
                for which in range(3):
                    halo_copy(m, which, d, dr, dc).wait_recv()

        second_norm = g1 * p2f[m].astype(F32) + b1
        c2[...] = jnp.where(second_norm + xf[m].astype(F32) > 0, g1, 0.0)
        first_norm = g0 * p1f[m, pl.ds(1, rows + 2)].astype(F32) + b0
        c1[...] = jnp.where((first_norm > 0) & valid, g0, 0.0)

        for d, (dr, dc) in enumerate(SPREAD):
            if (dr, dc) == (0, 0):

                @pl.when(s < sections - 1)
                def _():
                    section_copy(m, d, dr, dc).wait_recv()
            else:

                @pl.when(inside(-dr, -dc))
                def _():
                    section_copy(m, d, dr, dc).wait_recv()

        incoming = gf[m].astype(F32)
        second_grad = (incoming * c2[...]).astype(BF16).astype(F32)
        acc = None
        moved = wrapped(second_grad)
        base = m * rows * cols
        for i in range(3):
            for j in range(3):
                k = 3 * i + j
                part = moved[j][i : i + rows + 2]
                if not paired:
                    cols2[pl.ds(base, rows * cols), pl.ds(k * width, width)] = part[
                        1 : rows + 1, :cols
                    ].reshape(rows * cols, width)
                term = jnp.dot(
                    part.reshape((rows + 2) * pitch, width),
                    kt[1, pl.ds(k * width, width), :],
                    preferred_element_type=F32,
                )
                acc = term if acc is None else acc + term
        first_grad = (acc.reshape(rows + 2, pitch, width) * c1[...]).astype(BF16).astype(F32)
        if paired:
            second_own = second_grad[1 : rows + 3, :cols]
            first_own = first_grad[:, :cols]
            union_g[m, :, own] = jnp.where(c == 0, first_own, second_own).astype(BF16)
            spare_g[m] = jnp.where(c == 0, second_own, first_own).astype(BF16)
            pair_copy(m, 1, *pairs[1]).start()
        moved = wrapped(first_grad)
        for i in range(3):
            for j in range(3):
                k = 3 * i + j
                cols1[pl.ds(base, rows * cols), pl.ds(k * width, width)] = moved[j][
                    i : i + rows, :cols
                ].reshape(rows * cols, width)
        back = jnp.dot(
            cols1[pl.ds(base, rows * cols), :], kt[0], preferred_element_type=F32
        )
        tile = (pl.ds(2, rows), pl.ds(0, cols))
        masked = jnp.where(c2[tile] > 0, gf[(m, *tile)].astype(F32), 0.0)
        out_ref[m] = (masked + back.reshape(rows, cols, width)).astype(BF16)
        for d, (dr, dc) in enumerate(SPREAD):

            @pl.when((s > 0) & inside(dr, dc))
            def _():
                section_copy(m, d, dr, dc).start()

    if paired:
        area = rows * pitch
        edge = lax.broadcasted_iota(jnp.int32, (rows + 2, pitch, width), 1)
        for m in range(micros):
            for which in range(2):
                pair_arrival(m, which, *pairs[which]).wait_recv()
            field = union_g[m].astype(F32)
            moved = (
                jnp.where(edge > 0, pltpu.roll(field, 1, 1), 0.0).astype(BF16),
                union_g[m],
                jnp.where(edge < pitch - 1, pltpu.roll(field, pitch - 1, 1), 0.0).astype(BF16),
            )
            for i in range(3):
                for j in range(3):
                    cols2[
                        pl.ds(m * area, area), pl.ds((3 * i + j) * width, width)
                    ] = moved[j][i : i + rows].reshape(area, width)
        total = lax.dot_general(
            union_x[...].reshape(micros * area, width), cols2[...],
            (((0,), (0,)), ((), ())), preferred_element_type=F32,
        )
        for k in range(9):
            red[pl.ds((8 - k) * width, width), :] = (
                total[:, k * width : (k + 1) * width] * factor
            ).astype(BF16)

        def row_piece(index):
            return pl.ds(pl.multiple_of(index * chunk, 16), chunk)

        def out_piece(conv, index):
            return pl.ds(pl.multiple_of((conv * rows_n + index) * chunk, 16), chunk)

        def row_copy(step, src, dst, send, recv):
            peer = lax.rem(r + step + 1, rows_n)
            return pltpu.make_async_remote_copy(
                src_ref=red.at[row_piece(peer)] if src is red else src, dst_ref=dst.at[step],
                send_sem=send.at[step], recv_sem=recv.at[step],
                device_id=dev(s, peer, c), device_id_type=MESH,
            )

        def cross_copy(step):
            return pltpu.make_async_remote_copy(
                src_ref=gathered.at[step] if step < rows_n - 1 else final,
                dst_ref=crossed.at[step],
                send_sem=rs_send.at[rows_n + step], recv_sem=rs_recv.at[rows_n + step],
                device_id=dev(s, r, 1 - c), device_id_type=MESH,
            )

        def sum_copy(step):
            return row_copy(step, red, inbox, rs_send, rs_recv)

        def spread_copy(step):
            return row_copy(step, final, gathered, ag_send, ag_recv)

        for step in range(rows_n - 1):
            sum_copy(step).start()
        summed = red[row_piece(r), :].astype(F32)
        for step in range(rows_n - 1):
            sum_copy(step).wait_recv()
            summed = summed + inbox[step].astype(F32)
        final[...] = summed.astype(BF16)
        for step in range(rows_n - 1):
            spread_copy(step).start()
        cross_copy(rows_n - 1).start()
        fg_ref[out_piece(c, r), :] = final[...].astype(F32)
        for step in range(rows_n - 1):
            spread_copy(step).wait_recv()
            cross_copy(step).start()
            source = lax.rem(r + rows_n - step - 1, rows_n)
            fg_ref[out_piece(c, source), :] = gathered[step].astype(F32)
        for step in [rows_n - 1, *range(rows_n - 1)]:
            cross_copy(step).wait_recv()
            source = lax.rem(r + 2 * rows_n - step - 1, rows_n)
            fg_ref[out_piece(1 - c, source), :] = crossed[step].astype(F32)
        for step in range(rows_n - 1):
            sum_copy(step).wait_send()
            spread_copy(step).wait_send()
        for step in range(rows_n):
            cross_copy(step).wait_send()
        for m in range(micros):
            for which in range(2):
                pair_copy(m, which, *pairs[which]).wait_send()
    else:
        if red.shape[0] > 18 * width:
            red[pl.ds(18 * width, red.shape[0] - 18 * width), :] = jnp.zeros(
                (red.shape[0] - 18 * width, width), BF16
            )
        pixels = micros * rows * cols
        contract = (((0,), (0,)), ((), ()))
        inputs = xf[:, 2 : rows + 2, :cols].reshape(pixels, width)
        fields = (inputs, act[...])
        for conv, grads in ((1, cols2), (0, cols1)):
            total = lax.dot_general(fields[conv], grads[...], contract, preferred_element_type=F32)
            for k in range(9):
                red[pl.ds((conv * 9 + 8 - k) * width, width), :] = (
                    total[:, k * width : (k + 1) * width] * factor
                ).astype(BF16)

        def piece(index):
            return pl.ds(pl.multiple_of(index * chunk, 16), chunk)

        def peer_of(step):
            peer = lax.rem(me + step + 1, group)
            return peer, dev(s, peer // cols_n, lax.rem(peer, cols_n))

        def rs_copy(step):
            peer, where = peer_of(step)
            return pltpu.make_async_remote_copy(
                src_ref=red.at[piece(peer)], dst_ref=inbox.at[step],
                send_sem=rs_send.at[step], recv_sem=rs_recv.at[step],
                device_id=where, device_id_type=MESH,
            )

        def ag_copy(step):
            peer, where = peer_of(step)
            return pltpu.make_async_remote_copy(
                src_ref=final, dst_ref=gathered.at[step],
                send_sem=ag_send.at[step], recv_sem=ag_recv.at[step],
                device_id=where, device_id_type=MESH,
            )

        each(group - 1, lambda step: rs_copy(step).start())
        fg_ref[piece(me), :] = red[piece(me), :].astype(F32)

        def gather_in(step):
            rs_copy(step).wait_recv()
            fg_ref[piece(me), :] += inbox[step].astype(F32)

        each(group - 1, gather_in)
        final[...] = fg_ref[piece(me), :].astype(BF16)
        each(group - 1, lambda step: ag_copy(step).start())

        def spread_out(step):
            ag_copy(step).wait_recv()
            source = lax.rem(me + group - step - 1, group)
            fg_ref[piece(source), :] = gathered[step].astype(F32)

        each(group - 1, spread_out)

        each(group - 1, lambda step: rs_copy(step).wait_send())
        each(group - 1, lambda step: ag_copy(step).wait_send())
    for m in range(micros):
        for d, (dr, dc) in enumerate(SPREAD):
            if (dr, dc) != (0, 0):

                @pl.when(inside(dr, dc))
                def _():
                    for which in range(3):
                        halo_copy(m, which, d, dr, dc).wait_send()

                @pl.when(inside(dr, dc) & (s == sections - 1))
                def _():
                    out_grad_copy(m, d, dr, dc).wait_send()

            @pl.when((s > 0) & inside(dr, dc))
            def _():
                section_copy(m, d, dr, dc).wait_send()


def on_device(axes, sizes, section_input, first_pre, second_pre, out_grad, kernels, bn_scale, bn_shift):
    sections, rows_n, cols_n = sizes
    micros, rows, cols, width = out_grad.shape
    group = rows_n * cols_n
    tiles = 18 * width // 16
    chunk = 16 * (-(-tiles // group))
    pixels = micros * rows * cols
    factor = 1.0 / (pixels * group) ** 0.5
    paired = cols_n == 2 and tiles % group == 0
    dims = (axes, sections, rows_n, cols_n, factor, paired)
    pitch = 2 * cols
    dma = pltpu.SemaphoreType.DMA
    vmem = pl.BlockSpec(memory_space=pltpu.VMEM)
    field = pltpu.VMEM((micros, rows + 4, pitch, width), BF16)
    peers = max(group - 1, 1)
    wide = micros * rows * pitch if paired else pixels
    hbm = pl.BlockSpec(memory_space=pltpu.HBM)
    out, grads = pl.pallas_call(
        functools.partial(kernel, dims),
        out_shape=(
            jax.ShapeDtypeStruct(out_grad.shape, BF16),
            jax.ShapeDtypeStruct((group * chunk, width), F32),
        ),
        in_specs=[hbm] * 7,
        out_specs=(vmem, vmem),
        scratch_shapes=[
            field, field, field, field,
            pltpu.VMEM((2, 9, width, width), BF16),
            pltpu.VMEM((2, width), F32),
            pltpu.VMEM((2, width), F32),
            pltpu.VMEM((2, 9 * width, width), BF16),
            pltpu.VMEM((rows + 2, pitch, width), F32),
            pltpu.VMEM((rows + 4, pitch, width), F32),
            pltpu.VMEM((pixels, 9 * width), BF16),
            pltpu.VMEM((wide, 9 * width), BF16),
            pltpu.VMEM((pixels, width), BF16),
            pltpu.VMEM((micros, rows, pitch, width), BF16),
            pltpu.VMEM((micros, rows + 2, pitch, width), BF16),
            pltpu.VMEM((micros, rows, cols, width), BF16),
            pltpu.VMEM((micros, rows + 2, cols, width), BF16),
            pltpu.VMEM((rows_n, chunk, width), BF16),
            pltpu.VMEM((group * chunk, width), BF16),
            pltpu.VMEM((peers, chunk, width), BF16),
            pltpu.VMEM((chunk, width), BF16),
            pltpu.VMEM((peers, chunk, width), BF16),
            dma((7,)), dma((micros, 2)), dma((micros, 2)),
            dma((micros, 3, 9)), dma((micros, 3, 9)),
            dma((micros, 9)), dma((micros, 9)), dma((micros, 9)),
            dma((group + rows_n,)), dma((group + rows_n,)), dma((peers,)), dma((peers,)),
        ],
        compiler_params=pltpu.CompilerParams(
            collective_id=0, has_side_effects=True, vmem_limit_bytes=40 * 1024 * 1024
        ),
    )(
        section_input[0], first_pre[0], second_pre[0], out_grad,
        kernels[0].reshape(2, 9, width, width), bn_scale[0], bn_shift[0],
    )
    grads = grads[: 18 * width].reshape(1, 2, 3, 3, width, width)
    return out[None], grads


def solution(mesh):
    in_specs = (
        P("section", None, "row", "col", None),
        P("section", None, "row", "col", None),
        P("section", None, "row", "col", None),
        P(None, "row", "col", None),
        P("section", None, None, None, None, None),
        P("section", None, None),
        P("section", None, None),
    )
    out_specs = (P("section", None, "row", "col", None), P("section", None, None, None, None, None))
    sizes = tuple(mesh.shape[a] for a in ("section", "row", "col"))
    return jax.shard_map(
        functools.partial(on_device, tuple(mesh.axis_names), sizes),
        mesh=mesh, in_specs=in_specs, out_specs=out_specs, check_vma=False,
    )
```

```python
import functools

import jax
import jax.numpy as jnp
from jax import lax
from jax.experimental import pallas as pl
from jax.experimental.pallas import tpu as pltpu
from jax.sharding import PartitionSpec as P

MESH = pl.DeviceIdType.MESH
SPREAD = [(dr, dc) for dr in (-1, 0, 1) for dc in (-1, 0, 1)]
F32 = jnp.float32
BF16 = jnp.bfloat16


def each(count, body):
    if count <= 16:
        for step in range(count):
            body(step)
    else:

        def run(step, carry):
            body(step)
            return carry

        lax.fori_loop(0, count, run, 0)


def kernel(
    dims, x_ref, p1_ref, p2_ref, og_ref, k_hbm, scale_hbm, shift_hbm,
    out_hbm, fg_hbm,
    out_ref, fg_ref, xf, p1f, p2f, gf, k_ref, scale_ref, shift_ref, kt, c1, c2, cols1, cols2, act,
    union_x, union_g, spare_x, spare_g, crossed, red, inbox, final, gathered,
    stores, local, pair_send, pair_recv, halo_send, halo_recv, og_send, g_send, g_recv, rs_send, rs_recv, ag_send, ag_recv,
):
    axes, sections, rows_n, cols_n, factor, paired = dims
    micros, rows, cols, width = x_ref.shape
    pitch = 2 * cols
    half = cols // 2
    group = rows_n * cols_n
    chunk = final.shape[0]
    s = lax.axis_index("section")
    r = lax.axis_index("row")
    c = lax.axis_index("col")
    me = r * cols_n + c

    def dev(sec, row, col):
        where = {"section": sec, "row": row, "col": col}
        return tuple(where[a] for a in axes)

    def inside(dr, dc):
        return (r + dr >= 0) & (r + dr < rows_n) & (c + dc >= 0) & (c + dc < cols_n)

    def src_part(dr, dc):
        row = {-1: pl.ds(0, 2), 0: pl.ds(0, rows), 1: pl.ds(rows - 2, 2)}[dr]
        col = {-1: pl.ds(0, half), 0: pl.ds(0, cols), 1: pl.ds(half, half)}[dc]
        return row, col

    def dst_part(dr, dc):
        row = {-1: pl.ds(rows + 2, 2), 0: pl.ds(2, rows), 1: pl.ds(0, 2)}[dr]
        col = {-1: pl.ds(cols, half), 0: pl.ds(0, cols), 1: pl.ds(cols + half, half)}[dc]
        return row, col

    def shift_copy(src, dst, m, dr, dc, send, recv, sec):
        a, b = src_part(dr, dc)
        p, q = dst_part(dr, dc)
        if src is dst:
            a = pl.ds(a.start + 2, a.size)
        return pltpu.make_async_remote_copy(
            src_ref=src.at[m, a, b], dst_ref=dst.at[m, p, q],
            send_sem=send, recv_sem=recv,
            device_id=dev(sec, r + dr, c + dc), device_id_type=MESH,
        )

    def centre(ref):
        return ref.at[:, pl.ds(2, rows), pl.ds(0, cols)]

    loads = [
        pltpu.make_async_copy(src, dst, local.at[i])
        for i, (src, dst) in enumerate(
            (
                (p2_ref, centre(p2f)), (x_ref, centre(xf)), (p1_ref, centre(p1f)),
                (scale_hbm, scale_ref), (shift_hbm, shift_ref), (k_hbm, k_ref),
            )
        )
    ]
    og_load = pltpu.make_async_copy(og_ref, centre(gf), local.at[6])

    @pl.when(s == sections - 1)
    def _():
        og_load.start()

    for load in loads:
        load.start()

    for ref in (xf, p1f, p2f, gf):
        for m in range(micros):
            ref[m, 0:2] = jnp.zeros((2, pitch, width), BF16)
            ref[m, rows + 2 : rows + 4] = jnp.zeros((2, pitch, width), BF16)
            ref[m, 2 : rows + 2, cols:pitch] = jnp.zeros((rows, cols, width), BF16)

    barrier = pltpu.get_barrier_semaphore()

    def greet(step):
        peer = lax.rem(me + step + 1, group)
        pl.semaphore_signal(
            barrier, inc=1, device_id=dev(s, peer // cols_n, lax.rem(peer, cols_n)),
            device_id_type=MESH,
        )

    each(group - 1, greet)
    expected = group - 1 + jnp.int32(0)
    for dr, dc in SPREAD:
        expected = expected + jnp.where((s > 0) & inside(dr, dc), 1, 0)

        @pl.when((s < sections - 1) & inside(dr, dc))
        def _():
            pl.semaphore_signal(
                barrier, inc=1, device_id=dev(s + 1, r + dr, c + dc), device_id_type=MESH
            )

    for load in loads[:3]:
        load.wait()

    @pl.when(s == sections - 1)
    def _():
        og_load.wait()

    pl.semaphore_wait(barrier, expected)

    halos = ((p2f, p2f), (xf, xf), (p1f, p1f))
    around = [(d, dr, dc) for d, (dr, dc) in enumerate(SPREAD) if (dr, dc) != (0, 0)]

    def halo_copy(m, which, d, dr, dc):
        src, dst = halos[which]
        return shift_copy(
            src, dst, m, dr, dc, halo_send.at[m, which, d], halo_recv.at[m, which, d], s
        )

    def out_grad_copy(m, d, dr, dc):
        return shift_copy(gf, gf, m, dr, dc, og_send.at[m, d], g_recv.at[m, d], s)

    def section_copy(m, d, dr, dc):
        return shift_copy(
            out_ref, gf, m, dr, dc, g_send.at[m, d], g_recv.at[m, d], s - 1
        )

    for m in range(micros):
        for d, dr, dc in around:

            @pl.when(inside(dr, dc) & (s == sections - 1))
            def _():
                out_grad_copy(m, d, dr, dc).start()

            @pl.when(inside(dr, dc))
            def _():
                for which in range(3):
                    halo_copy(m, which, d, dr, dc).start()

    for load in loads[3:]:
        load.wait()
    for conv in range(2):
        for k in range(9):
            kt[conv, pl.ds(k * width, width), :] = jnp.transpose(k_ref[conv, 8 - k])

    g0 = scale_ref[0:1, :].reshape(1, 1, width)
    g1 = scale_ref[1:2, :].reshape(1, 1, width)
    b0 = shift_ref[0:1, :].reshape(1, 1, width)
    b1 = shift_ref[1:2, :].reshape(1, 1, width)
    own = pl.ds(pl.multiple_of(c * cols, cols), cols)

    def pair_copy(m, which, src, dst):
        return pltpu.make_async_remote_copy(
            src_ref=src.at[m], dst_ref=dst.at[m, :, own],
            send_sem=pair_send.at[m, which], recv_sem=pair_recv.at[m, which],
            device_id=dev(s, r, 1 - c), device_id_type=MESH,
        )

    def pair_arrival(m, which, src, dst):
        other = pl.ds(pl.multiple_of((1 - c) * cols, cols), cols)
        return pltpu.make_async_remote_copy(
            src_ref=src.at[m], dst_ref=dst.at[m, :, other],
            send_sem=pair_send.at[m, which], recv_sem=pair_recv.at[m, which],
            device_id=dev(s, r, 1 - c), device_id_type=MESH,
        )

    pairs = ((spare_x, union_x), (spare_g, union_g))
    for m in range(micros):
        first_norm = g0 * p1f[m, 2 : rows + 2, :cols].astype(F32) + b0
        active = jnp.maximum(first_norm, 0.0)
        if paired:
            inputs = xf[m, 2 : rows + 2, :cols].astype(F32)
            union_x[m, :, own] = jnp.where(c == 0, inputs, active).astype(BF16)
            spare_x[m] = jnp.where(c == 0, active, inputs).astype(BF16)
            pair_copy(m, 0, *pairs[0]).start()
        else:
            act[pl.ds(m * rows * cols, rows * cols), :] = active.astype(BF16).reshape(
                rows * cols, width
            )

    row_i = lax.broadcasted_iota(jnp.int32, (rows + 2, pitch, width), 0)
    col_i = lax.broadcasted_iota(jnp.int32, (rows + 2, pitch, width), 1)
    row_lo = jnp.where(r == 0, 1, 0)
    row_hi = jnp.where(r == rows_n - 1, rows, rows + 1)
    col_hi = jnp.where(c == cols_n - 1, cols, cols + half)
    col_lo = jnp.where(c == 0, pitch, cols + half)
    valid = (
        (row_i >= row_lo) & (row_i <= row_hi) & ((col_i < col_hi) | (col_i >= col_lo))
    )

    def wrapped(field):
        left = pltpu.roll(field, 1, 1)
        right = pltpu.roll(field, pitch - 1, 1)
        return left.astype(BF16), field.astype(BF16), right.astype(BF16)

    def out_store(m):
        return pltpu.make_async_copy(out_ref.at[m], out_hbm.at[m], stores.at[m])

    def grad_store(index):
        rows_at = pl.ds(pl.multiple_of(index * chunk, 16), chunk)
        return pltpu.make_async_copy(
            fg_ref.at[rows_at], fg_hbm.at[rows_at], stores.at[micros + index]
        )

    for m in range(micros):
        for d, dr, dc in around:

            @pl.when(inside(-dr, -dc))
            def _():
                for which in range(3):
                    halo_copy(m, which, d, dr, dc).wait_recv()

        second_norm = g1 * p2f[m].astype(F32) + b1
        c2[...] = jnp.where(second_norm + xf[m].astype(F32) > 0, g1, 0.0)
        first_norm = g0 * p1f[m, pl.ds(1, rows + 2)].astype(F32) + b0
        c1[...] = jnp.where((first_norm > 0) & valid, g0, 0.0)

        for d, (dr, dc) in enumerate(SPREAD):
            if (dr, dc) == (0, 0):

                @pl.when(s < sections - 1)
                def _():
                    section_copy(m, d, dr, dc).wait_recv()
            else:

                @pl.when(inside(-dr, -dc))
                def _():
                    section_copy(m, d, dr, dc).wait_recv()

        incoming = gf[m].astype(F32)
        second_grad = (incoming * c2[...]).astype(BF16).astype(F32)
        acc = None
        moved = wrapped(second_grad)
        base = m * rows * cols
        for i in range(3):
            for j in range(3):
                k = 3 * i + j
                part = moved[j][i : i + rows + 2]
                if not paired:
                    cols2[pl.ds(base, rows * cols), pl.ds(k * width, width)] = part[
                        1 : rows + 1, :cols
                    ].reshape(rows * cols, width)
                term = jnp.dot(
                    part.reshape((rows + 2) * pitch, width),
                    kt[1, pl.ds(k * width, width), :],
                    preferred_element_type=F32,
                )
                acc = term if acc is None else acc + term
        first_grad = (acc.reshape(rows + 2, pitch, width) * c1[...]).astype(BF16).astype(F32)
        if paired:
            second_own = second_grad[1 : rows + 3, :cols]
            first_own = first_grad[:, :cols]
            union_g[m, :, own] = jnp.where(c == 0, first_own, second_own).astype(BF16)
            spare_g[m] = jnp.where(c == 0, second_own, first_own).astype(BF16)
            pair_copy(m, 1, *pairs[1]).start()
        moved = wrapped(first_grad)
        for i in range(3):
            for j in range(3):
                k = 3 * i + j
                cols1[pl.ds(base, rows * cols), pl.ds(k * width, width)] = moved[j][
                    i : i + rows, :cols
                ].reshape(rows * cols, width)
        back = jnp.dot(
            cols1[pl.ds(base, rows * cols), :], kt[0], preferred_element_type=F32
        )
        tile = (pl.ds(2, rows), pl.ds(0, cols))
        masked = jnp.where(c2[tile] > 0, gf[(m, *tile)].astype(F32), 0.0)
        out_ref[m] = (masked + back.reshape(rows, cols, width)).astype(BF16)
        out_store(m).start()
        for d, (dr, dc) in enumerate(SPREAD):

            @pl.when((s > 0) & inside(dr, dc))
            def _():
                section_copy(m, d, dr, dc).start()

    if paired:
        area = rows * pitch
        edge = lax.broadcasted_iota(jnp.int32, (rows + 2, pitch, width), 1)
        for m in range(micros):
            for which in range(2):
                pair_arrival(m, which, *pairs[which]).wait_recv()
            field = union_g[m].astype(F32)
            moved = (
                jnp.where(edge > 0, pltpu.roll(field, 1, 1), 0.0).astype(BF16),
                union_g[m],
                jnp.where(edge < pitch - 1, pltpu.roll(field, pitch - 1, 1), 0.0).astype(BF16),
            )
            for i in range(3):
                for j in range(3):
                    cols2[
                        pl.ds(m * area, area), pl.ds((3 * i + j) * width, width)
                    ] = moved[j][i : i + rows].reshape(area, width)
        total = lax.dot_general(
            union_x[...].reshape(micros * area, width), cols2[...],
            (((0,), (0,)), ((), ())), preferred_element_type=F32,
        )
        for k in range(9):
            red[pl.ds((8 - k) * width, width), :] = (
                total[:, k * width : (k + 1) * width] * factor
            ).astype(BF16)

        def row_piece(index):
            return pl.ds(pl.multiple_of(index * chunk, 16), chunk)

        def out_piece(conv, index):
            return pl.ds(pl.multiple_of((conv * rows_n + index) * chunk, 16), chunk)

        def row_copy(step, src, dst, send, recv):
            peer = lax.rem(r + step + 1, rows_n)
            return pltpu.make_async_remote_copy(
                src_ref=red.at[row_piece(peer)] if src is red else src, dst_ref=dst.at[step],
                send_sem=send.at[step], recv_sem=recv.at[step],
                device_id=dev(s, peer, c), device_id_type=MESH,
            )

        def cross_copy(step):
            return pltpu.make_async_remote_copy(
                src_ref=gathered.at[step] if step < rows_n - 1 else final,
                dst_ref=crossed.at[step],
                send_sem=rs_send.at[rows_n + step], recv_sem=rs_recv.at[rows_n + step],
                device_id=dev(s, r, 1 - c), device_id_type=MESH,
            )

        def sum_copy(step):
            return row_copy(step, red, inbox, rs_send, rs_recv)

        def spread_copy(step):
            return row_copy(step, final, gathered, ag_send, ag_recv)

        for step in range(rows_n - 1):
            sum_copy(step).start()
        summed = red[row_piece(r), :].astype(F32)
        for step in range(rows_n - 1):
            sum_copy(step).wait_recv()
            summed = summed + inbox[step].astype(F32)
        final[...] = summed.astype(BF16)
        for step in range(rows_n - 1):
            spread_copy(step).start()
        cross_copy(rows_n - 1).start()
        fg_ref[out_piece(c, r), :] = final[...].astype(F32)
        grad_store(c * rows_n + r).start()
        for step in range(rows_n - 1):
            spread_copy(step).wait_recv()
            cross_copy(step).start()
            source = lax.rem(r + rows_n - step - 1, rows_n)
            fg_ref[out_piece(c, source), :] = gathered[step].astype(F32)
            grad_store(c * rows_n + source).start()
        for step in [rows_n - 1, *range(rows_n - 1)]:
            cross_copy(step).wait_recv()
            source = lax.rem(r + 2 * rows_n - step - 1, rows_n)
            fg_ref[out_piece(1 - c, source), :] = crossed[step].astype(F32)
            grad_store((1 - c) * rows_n + source).start()
        for step in range(rows_n - 1):
            sum_copy(step).wait_send()
            spread_copy(step).wait_send()
        for step in range(rows_n):
            cross_copy(step).wait_send()
        for m in range(micros):
            for which in range(2):
                pair_copy(m, which, *pairs[which]).wait_send()
    else:
        if red.shape[0] > 18 * width:
            red[pl.ds(18 * width, red.shape[0] - 18 * width), :] = jnp.zeros(
                (red.shape[0] - 18 * width, width), BF16
            )
        pixels = micros * rows * cols
        contract = (((0,), (0,)), ((), ()))
        inputs = xf[:, 2 : rows + 2, :cols].reshape(pixels, width)
        fields = (inputs, act[...])
        for conv, grads in ((1, cols2), (0, cols1)):
            total = lax.dot_general(fields[conv], grads[...], contract, preferred_element_type=F32)
            for k in range(9):
                red[pl.ds((conv * 9 + 8 - k) * width, width), :] = (
                    total[:, k * width : (k + 1) * width] * factor
                ).astype(BF16)

        def piece(index):
            return pl.ds(pl.multiple_of(index * chunk, 16), chunk)

        def peer_of(step):
            peer = lax.rem(me + step + 1, group)
            return peer, dev(s, peer // cols_n, lax.rem(peer, cols_n))

        def rs_copy(step):
            peer, where = peer_of(step)
            return pltpu.make_async_remote_copy(
                src_ref=red.at[piece(peer)], dst_ref=inbox.at[step],
                send_sem=rs_send.at[step], recv_sem=rs_recv.at[step],
                device_id=where, device_id_type=MESH,
            )

        def ag_copy(step):
            peer, where = peer_of(step)
            return pltpu.make_async_remote_copy(
                src_ref=final, dst_ref=gathered.at[step],
                send_sem=ag_send.at[step], recv_sem=ag_recv.at[step],
                device_id=where, device_id_type=MESH,
            )

        each(group - 1, lambda step: rs_copy(step).start())
        fg_ref[piece(me), :] = red[piece(me), :].astype(F32)

        def gather_in(step):
            rs_copy(step).wait_recv()
            fg_ref[piece(me), :] += inbox[step].astype(F32)

        each(group - 1, gather_in)
        final[...] = fg_ref[piece(me), :].astype(BF16)
        each(group - 1, lambda step: ag_copy(step).start())

        def spread_out(step):
            ag_copy(step).wait_recv()
            source = lax.rem(me + group - step - 1, group)
            fg_ref[piece(source), :] = gathered[step].astype(F32)

        each(group - 1, spread_out)

        each(group, lambda step: grad_store(step).start())
        each(group - 1, lambda step: rs_copy(step).wait_send())
        each(group - 1, lambda step: ag_copy(step).wait_send())
    each(group, lambda step: grad_store(step).wait())
    for m in range(micros):
        out_store(m).wait()
    for m in range(micros):
        for d, (dr, dc) in enumerate(SPREAD):
            if (dr, dc) != (0, 0):

                @pl.when(inside(dr, dc))
                def _():
                    for which in range(3):
                        halo_copy(m, which, d, dr, dc).wait_send()

                @pl.when(inside(dr, dc) & (s == sections - 1))
                def _():
                    out_grad_copy(m, d, dr, dc).wait_send()

            @pl.when((s > 0) & inside(dr, dc))
            def _():
                section_copy(m, d, dr, dc).wait_send()


def on_device(axes, sizes, section_input, first_pre, second_pre, out_grad, kernels, bn_scale, bn_shift):
    sections, rows_n, cols_n = sizes
    micros, rows, cols, width = out_grad.shape
    group = rows_n * cols_n
    tiles = 18 * width // 16
    chunk = 16 * (-(-tiles // group))
    pixels = micros * rows * cols
    factor = 1.0 / (pixels * group) ** 0.5
    paired = cols_n == 2 and tiles % group == 0
    dims = (axes, sections, rows_n, cols_n, factor, paired)
    pitch = 2 * cols
    dma = pltpu.SemaphoreType.DMA
    field = pltpu.VMEM((micros, rows + 4, pitch, width), BF16)
    peers = max(group - 1, 1)
    wide = micros * rows * pitch if paired else pixels
    hbm = pl.BlockSpec(memory_space=pl.ANY)
    out, grads = pl.pallas_call(
        functools.partial(kernel, dims),
        out_shape=(
            jax.ShapeDtypeStruct(out_grad.shape, BF16),
            jax.ShapeDtypeStruct((group * chunk, width), F32),
        ),
        in_specs=[hbm] * 7,
        out_specs=(hbm, hbm),
        scratch_shapes=[
            pltpu.VMEM(out_grad.shape, BF16),
            pltpu.VMEM((group * chunk, width), F32),
            field, field, field, field,
            pltpu.VMEM((2, 9, width, width), BF16),
            pltpu.VMEM((2, width), F32),
            pltpu.VMEM((2, width), F32),
            pltpu.VMEM((2, 9 * width, width), BF16),
            pltpu.VMEM((rows + 2, pitch, width), F32),
            pltpu.VMEM((rows + 4, pitch, width), F32),
            pltpu.VMEM((pixels, 9 * width), BF16),
            pltpu.VMEM((wide, 9 * width), BF16),
            pltpu.VMEM((pixels, width), BF16),
            pltpu.VMEM((micros, rows, pitch, width), BF16),
            pltpu.VMEM((micros, rows + 2, pitch, width), BF16),
            pltpu.VMEM((micros, rows, cols, width), BF16),
            pltpu.VMEM((micros, rows + 2, cols, width), BF16),
            pltpu.VMEM((rows_n, chunk, width), BF16),
            pltpu.VMEM((group * chunk, width), BF16),
            pltpu.VMEM((peers, chunk, width), BF16),
            pltpu.VMEM((chunk, width), BF16),
            pltpu.VMEM((peers, chunk, width), BF16),
            dma((micros + group,)), dma((7,)), dma((micros, 2)), dma((micros, 2)),
            dma((micros, 3, 9)), dma((micros, 3, 9)),
            dma((micros, 9)), dma((micros, 9)), dma((micros, 9)),
            dma((group + rows_n,)), dma((group + rows_n,)), dma((peers,)), dma((peers,)),
        ],
        compiler_params=pltpu.CompilerParams(
            collective_id=0, has_side_effects=True, vmem_limit_bytes=62 * 1024 * 1024
        ),
    )(
        section_input[0], first_pre[0], second_pre[0], out_grad,
        kernels[0].reshape(2, 9, width, width), bn_scale[0], bn_shift[0],
    )
    grads = grads[: 18 * width].reshape(1, 2, 3, 3, width, width)
    return out[None], grads


def solution(mesh):
    in_specs = (
        P("section", None, "row", "col", None),
        P("section", None, "row", "col", None),
        P("section", None, "row", "col", None),
        P(None, "row", "col", None),
        P("section", None, None, None, None, None),
        P("section", None, None),
        P("section", None, None),
    )
    out_specs = (P("section", None, "row", "col", None), P("section", None, None, None, None, None))
    sizes = tuple(mesh.shape[a] for a in ("section", "row", "col"))
    return jax.shard_map(
        functools.partial(on_device, tuple(mesh.axis_names), sizes),
        mesh=mesh, in_specs=in_specs, out_specs=out_specs, check_vma=False,
    )
```

```python
import functools

import jax
import jax.numpy as jnp
from jax import lax
from jax.experimental import pallas as pl
from jax.experimental.pallas import tpu as pltpu
from jax.sharding import PartitionSpec as P

MESH = pl.DeviceIdType.MESH
SPREAD = [(dr, dc) for dr in (-1, 0, 1) for dc in (-1, 0, 1)]
F32 = jnp.float32
BF16 = jnp.bfloat16


def each(count, body):
    if count <= 16:
        for step in range(count):
            body(step)
    else:

        def run(step, carry):
            body(step)
            return carry

        lax.fori_loop(0, count, run, 0)


def kernel(
    dims, x_ref, p1_ref, p2_ref, og_ref, k_hbm, scale_hbm, shift_hbm,
    out_hbm, fg_hbm,
    out_ref, fg_ref, xf, p1f, p2f, gf, k_ref, scale_ref, shift_ref, kt, c1, c2, cols1, cols2, act,
    union_x, union_g, spare_x, spare_g, crossed, parted, red, inbox, final, gathered,
    stores, local, pair_send, pair_recv, halo_send, halo_recv, og_send, g_send, g_recv, rs_send, rs_recv, ag_send, ag_recv,
):
    axes, sections, rows_n, cols_n, factor, paired, chunk_rows = dims
    micros, rows, cols, width = x_ref.shape
    pitch = 2 * cols
    half = cols // 2
    group = rows_n * cols_n
    chunk = chunk_rows
    s = lax.axis_index("section")
    r = lax.axis_index("row")
    c = lax.axis_index("col")
    me = r * cols_n + c

    def dev(sec, row, col):
        where = {"section": sec, "row": row, "col": col}
        return tuple(where[a] for a in axes)

    def inside(dr, dc):
        return (r + dr >= 0) & (r + dr < rows_n) & (c + dc >= 0) & (c + dc < cols_n)

    def src_part(dr, dc):
        row = {-1: pl.ds(0, 2), 0: pl.ds(0, rows), 1: pl.ds(rows - 2, 2)}[dr]
        col = {-1: pl.ds(0, half), 0: pl.ds(0, cols), 1: pl.ds(half, half)}[dc]
        return row, col

    def dst_part(dr, dc):
        row = {-1: pl.ds(rows + 2, 2), 0: pl.ds(2, rows), 1: pl.ds(0, 2)}[dr]
        col = {-1: pl.ds(cols, half), 0: pl.ds(0, cols), 1: pl.ds(cols + half, half)}[dc]
        return row, col

    def shift_copy(src, dst, m, dr, dc, send, recv, sec):
        a, b = src_part(dr, dc)
        p, q = dst_part(dr, dc)
        if src is dst:
            a = pl.ds(a.start + 2, a.size)
        return pltpu.make_async_remote_copy(
            src_ref=src.at[m, a, b], dst_ref=dst.at[m, p, q],
            send_sem=send, recv_sem=recv,
            device_id=dev(sec, r + dr, c + dc), device_id_type=MESH,
        )

    def centre(ref):
        return ref.at[:, pl.ds(2, rows), pl.ds(0, cols)]

    loads = [
        pltpu.make_async_copy(src, dst, local.at[i])
        for i, (src, dst) in enumerate(
            (
                (p2_ref, centre(p2f)), (x_ref, centre(xf)), (p1_ref, centre(p1f)),
                (scale_hbm, scale_ref), (shift_hbm, shift_ref), (k_hbm, k_ref),
            )
        )
    ]
    og_load = pltpu.make_async_copy(og_ref, centre(gf), local.at[6])

    @pl.when(s == sections - 1)
    def _():
        og_load.start()

    for load in loads:
        load.start()

    for ref in (xf, p1f, p2f, gf):
        for m in range(micros):
            ref[m, 0:2] = jnp.zeros((2, pitch, width), BF16)
            ref[m, rows + 2 : rows + 4] = jnp.zeros((2, pitch, width), BF16)
            ref[m, 2 : rows + 2, cols:pitch] = jnp.zeros((rows, cols, width), BF16)

    barrier = pltpu.get_barrier_semaphore()

    def greet(step):
        peer = lax.rem(me + step + 1, group)
        pl.semaphore_signal(
            barrier, inc=1, device_id=dev(s, peer // cols_n, lax.rem(peer, cols_n)),
            device_id_type=MESH,
        )

    each(group - 1, greet)
    expected = group - 1 + jnp.int32(0)
    for dr, dc in SPREAD:
        expected = expected + jnp.where((s > 0) & inside(dr, dc), 1, 0)

        @pl.when((s < sections - 1) & inside(dr, dc))
        def _():
            pl.semaphore_signal(
                barrier, inc=1, device_id=dev(s + 1, r + dr, c + dc), device_id_type=MESH
            )

    for load in loads[:3]:
        load.wait()

    @pl.when(s == sections - 1)
    def _():
        og_load.wait()

    pl.semaphore_wait(barrier, expected)

    halos = ((p2f, p2f), (xf, xf), (p1f, p1f))
    around = [(d, dr, dc) for d, (dr, dc) in enumerate(SPREAD) if (dr, dc) != (0, 0)]

    def halo_copy(m, which, d, dr, dc):
        src, dst = halos[which]
        return shift_copy(
            src, dst, m, dr, dc, halo_send.at[m, which, d], halo_recv.at[m, which, d], s
        )

    def out_grad_copy(m, d, dr, dc):
        return shift_copy(gf, gf, m, dr, dc, og_send.at[m, d], g_recv.at[m, d], s)

    def section_copy(m, d, dr, dc):
        return shift_copy(
            out_ref, gf, m, dr, dc, g_send.at[m, d], g_recv.at[m, d], s - 1
        )

    for m in range(micros):
        for d, dr, dc in around:

            @pl.when(inside(dr, dc) & (s == sections - 1))
            def _():
                out_grad_copy(m, d, dr, dc).start()

            @pl.when(inside(dr, dc))
            def _():
                for which in range(3):
                    halo_copy(m, which, d, dr, dc).start()

    for load in loads[3:]:
        load.wait()
    for conv in range(2):
        for k in range(9):
            kt[conv, pl.ds(k * width, width), :] = jnp.transpose(k_ref[conv, 8 - k])

    g0 = scale_ref[0:1, :].reshape(1, 1, width)
    g1 = scale_ref[1:2, :].reshape(1, 1, width)
    b0 = shift_ref[0:1, :].reshape(1, 1, width)
    b1 = shift_ref[1:2, :].reshape(1, 1, width)
    own = pl.ds(pl.multiple_of(c * cols, cols), cols)

    def pair_copy(m, which, src, dst):
        return pltpu.make_async_remote_copy(
            src_ref=src.at[m], dst_ref=dst.at[m, :, own],
            send_sem=pair_send.at[m, which], recv_sem=pair_recv.at[m, which],
            device_id=dev(s, r, 1 - c), device_id_type=MESH,
        )

    def pair_arrival(m, which, src, dst):
        other = pl.ds(pl.multiple_of((1 - c) * cols, cols), cols)
        return pltpu.make_async_remote_copy(
            src_ref=src.at[m], dst_ref=dst.at[m, :, other],
            send_sem=pair_send.at[m, which], recv_sem=pair_recv.at[m, which],
            device_id=dev(s, r, 1 - c), device_id_type=MESH,
        )

    pairs = ((spare_x, union_x), (spare_g, union_g))
    for m in range(micros):
        first_norm = g0 * p1f[m, 2 : rows + 2, :cols].astype(F32) + b0
        active = jnp.maximum(first_norm, 0.0)
        if paired:
            inputs = xf[m, 2 : rows + 2, :cols].astype(F32)
            union_x[m, :, own] = jnp.where(c == 0, inputs, active).astype(BF16)
            spare_x[m] = jnp.where(c == 0, active, inputs).astype(BF16)
            pair_copy(m, 0, *pairs[0]).start()
        else:
            act[pl.ds(m * rows * cols, rows * cols), :] = active.astype(BF16).reshape(
                rows * cols, width
            )

    row_i = lax.broadcasted_iota(jnp.int32, (rows + 2, pitch, width), 0)
    col_i = lax.broadcasted_iota(jnp.int32, (rows + 2, pitch, width), 1)
    row_lo = jnp.where(r == 0, 1, 0)
    row_hi = jnp.where(r == rows_n - 1, rows, rows + 1)
    col_hi = jnp.where(c == cols_n - 1, cols, cols + half)
    col_lo = jnp.where(c == 0, pitch, cols + half)
    valid = (
        (row_i >= row_lo) & (row_i <= row_hi) & ((col_i < col_hi) | (col_i >= col_lo))
    )

    def wrapped(field):
        left = pltpu.roll(field, 1, 1)
        right = pltpu.roll(field, pitch - 1, 1)
        return left.astype(BF16), field.astype(BF16), right.astype(BF16)

    def out_store(m):
        return pltpu.make_async_copy(out_ref.at[m], out_hbm.at[m], stores.at[m])

    for m in range(micros):
        for d, dr, dc in around:

            @pl.when(inside(-dr, -dc))
            def _():
                for which in range(3):
                    halo_copy(m, which, d, dr, dc).wait_recv()

        second_norm = g1 * p2f[m].astype(F32) + b1
        c2[...] = jnp.where(second_norm + xf[m].astype(F32) > 0, g1, 0.0)
        first_norm = g0 * p1f[m, pl.ds(1, rows + 2)].astype(F32) + b0
        c1[...] = jnp.where((first_norm > 0) & valid, g0, 0.0)

        for d, (dr, dc) in enumerate(SPREAD):
            if (dr, dc) == (0, 0):

                @pl.when(s < sections - 1)
                def _():
                    section_copy(m, d, dr, dc).wait_recv()
            else:

                @pl.when(inside(-dr, -dc))
                def _():
                    section_copy(m, d, dr, dc).wait_recv()

        incoming = gf[m].astype(F32)
        second_grad = (incoming * c2[...]).astype(BF16).astype(F32)
        acc = None
        moved = wrapped(second_grad)
        base = m * rows * cols
        for i in range(3):
            for j in range(3):
                k = 3 * i + j
                part = moved[j][i : i + rows + 2]
                if not paired:
                    cols2[pl.ds(base, rows * cols), pl.ds(k * width, width)] = part[
                        1 : rows + 1, :cols
                    ].reshape(rows * cols, width)
                term = jnp.dot(
                    part.reshape((rows + 2) * pitch, width),
                    kt[1, pl.ds(k * width, width), :],
                    preferred_element_type=F32,
                )
                acc = term if acc is None else acc + term
        first_grad = (acc.reshape(rows + 2, pitch, width) * c1[...]).astype(BF16).astype(F32)
        if paired:
            second_own = second_grad[1 : rows + 3, :cols]
            first_own = first_grad[:, :cols]
            union_g[m, :, own] = jnp.where(c == 0, first_own, second_own).astype(BF16)
            spare_g[m] = jnp.where(c == 0, second_own, first_own).astype(BF16)
            pair_copy(m, 1, *pairs[1]).start()
        moved = wrapped(first_grad)
        for i in range(3):
            for j in range(3):
                k = 3 * i + j
                cols1[pl.ds(base, rows * cols), pl.ds(k * width, width)] = moved[j][
                    i : i + rows, :cols
                ].reshape(rows * cols, width)
        back = jnp.dot(
            cols1[pl.ds(base, rows * cols), :], kt[0], preferred_element_type=F32
        )
        tile = (pl.ds(2, rows), pl.ds(0, cols))
        masked = jnp.where(c2[tile] > 0, gf[(m, *tile)].astype(F32), 0.0)
        out_ref[m] = (masked + back.reshape(rows, cols, width)).astype(BF16)
        out_store(m).start()
        for d, (dr, dc) in enumerate(SPREAD):

            @pl.when((s > 0) & inside(dr, dc))
            def _():
                section_copy(m, d, dr, dc).start()

    if paired:
        area = rows * pitch
        edge = lax.broadcasted_iota(jnp.int32, (rows + 2, pitch, width), 1)
        for m in range(micros):
            for which in range(2):
                pair_arrival(m, which, *pairs[which]).wait_recv()
            field = union_g[m].astype(F32)
            moved = (
                jnp.where(edge > 0, pltpu.roll(field, 1, 1), 0.0).astype(BF16),
                union_g[m],
                jnp.where(edge < pitch - 1, pltpu.roll(field, pitch - 1, 1), 0.0).astype(BF16),
            )
            for i in range(3):
                for j in range(3):
                    cols2[
                        pl.ds(m * area, area), pl.ds((3 * i + j) * width, width)
                    ] = moved[j][i : i + rows].reshape(area, width)
        total = lax.dot_general(
            union_x[...].reshape(micros * area, width), cols2[...],
            (((0,), (0,)), ((), ())), preferred_element_type=F32,
        )
        for k in range(9):
            red[pl.ds((8 - k) * width, width), :] = (
                total[:, k * width : (k + 1) * width] * factor
            ).astype(BF16)

        parts = parted.shape[0]
        sub = parted.shape[1]
        side = lax.rem(r, 2)
        beside = r + 1 - 2 * side
        across = lax.rem(r + 2, 4)

        def half_rows(which, q):
            return pl.ds(pl.multiple_of((which * parts + q) * sub, 16), sub)

        def send(src, dst, sem, where):
            return pltpu.make_async_remote_copy(
                src_ref=src, dst_ref=dst, send_sem=rs_send.at[sem], recv_sem=rs_recv.at[sem],
                device_id=where, device_id_type=MESH,
            )

        def beside_sum(q):
            return send(red.at[half_rows(1 - side, q)], inbox.at[q], q, dev(s, beside, c))

        def across_sum(q):
            return send(parted.at[q], inbox.at[parts + q], parts + q, dev(s, across, c))

        def beside_copy(q):
            return send(final.at[q], gathered.at[q], 2 * parts + q, dev(s, beside, c))

        def cross_copy(q):
            src = final.at[q] if q < parts else gathered.at[q - parts]
            return send(src, crossed.at[q], 3 * parts + q, dev(s, r, 1 - c))

        def grad_store(src, conv, which, q, slot):
            rows_at = pl.ds(
                pl.multiple_of(((conv * 2 + which) * parts + q) * sub, 16), sub
            )
            return pltpu.make_async_copy(src, fg_hbm.at[rows_at], stores.at[micros + slot])

        written = []
        for q in range(parts):
            beside_sum(q).start()
        for q in range(parts):
            beside_sum(q).wait_recv()
            parted[q] = (
                red[half_rows(side, q), :].astype(F32) + inbox[q].astype(F32)
            ).astype(BF16)
            across_sum(q).start()
        for q in range(parts):
            across_sum(q).wait_recv()
            final[q] = (parted[q].astype(F32) + inbox[parts + q].astype(F32)).astype(BF16)
            beside_copy(q).start()
            cross_copy(q).start()
            written.append(grad_store(final.at[q], c, side, q, q))
            written[-1].start()
        for q in range(parts):
            beside_copy(q).wait_recv()
            cross_copy(parts + q).start()
            written.append(grad_store(gathered.at[q], c, 1 - side, q, parts + q))
            written[-1].start()
        for q in range(2 * parts):
            cross_copy(q).wait_recv()
            which = side if q < parts else 1 - side
            written.append(
                grad_store(crossed.at[q], 1 - c, which, q % parts, 2 * parts + q)
            )
            written[-1].start()
        for q in range(parts):
            beside_sum(q).wait_send()
            across_sum(q).wait_send()
            beside_copy(q).wait_send()
        for q in range(2 * parts):
            cross_copy(q).wait_send()
        for store in written:
            store.wait()
        for m in range(micros):
            for which in range(2):
                pair_copy(m, which, *pairs[which]).wait_send()
    else:
        if red.shape[0] > 18 * width:
            red[pl.ds(18 * width, red.shape[0] - 18 * width), :] = jnp.zeros(
                (red.shape[0] - 18 * width, width), BF16
            )
        pixels = micros * rows * cols
        contract = (((0,), (0,)), ((), ()))
        inputs = xf[:, 2 : rows + 2, :cols].reshape(pixels, width)
        fields = (inputs, act[...])
        for conv, grads in ((1, cols2), (0, cols1)):
            total = lax.dot_general(fields[conv], grads[...], contract, preferred_element_type=F32)
            for k in range(9):
                red[pl.ds((conv * 9 + 8 - k) * width, width), :] = (
                    total[:, k * width : (k + 1) * width] * factor
                ).astype(BF16)

        def piece(index):
            return pl.ds(pl.multiple_of(index * chunk, 16), chunk)

        def peer_of(step):
            peer = lax.rem(me + step + 1, group)
            return peer, dev(s, peer // cols_n, lax.rem(peer, cols_n))

        def rs_copy(step):
            peer, where = peer_of(step)
            return pltpu.make_async_remote_copy(
                src_ref=red.at[piece(peer)], dst_ref=inbox.at[step],
                send_sem=rs_send.at[step], recv_sem=rs_recv.at[step],
                device_id=where, device_id_type=MESH,
            )

        def ag_copy(step):
            peer, where = peer_of(step)
            return pltpu.make_async_remote_copy(
                src_ref=final, dst_ref=gathered.at[step],
                send_sem=ag_send.at[step], recv_sem=ag_recv.at[step],
                device_id=where, device_id_type=MESH,
            )

        each(group - 1, lambda step: rs_copy(step).start())
        fg_ref[...] = red[piece(me), :].astype(F32)

        def gather_in(step):
            rs_copy(step).wait_recv()
            fg_ref[...] += inbox[step].astype(F32)

        each(group - 1, gather_in)
        final[...] = fg_ref[...].astype(BF16)

        def grad_store(src, index, slot):
            return pltpu.make_async_copy(
                src, fg_hbm.at[piece(index)], stores.at[micros + slot]
            )

        grad_store(final, me, group - 1).start()
        each(group - 1, lambda step: ag_copy(step).start())

        def spread_out(step):
            ag_copy(step).wait_recv()
            source = lax.rem(me + group - step - 1, group)
            grad_store(gathered.at[step], source, step).start()

        each(group - 1, spread_out)

        each(group, lambda step: grad_store(final, me, step).wait())
        each(group - 1, lambda step: rs_copy(step).wait_send())
        each(group - 1, lambda step: ag_copy(step).wait_send())
    for m in range(micros):
        out_store(m).wait()
    for m in range(micros):
        for d, (dr, dc) in enumerate(SPREAD):
            if (dr, dc) != (0, 0):

                @pl.when(inside(dr, dc))
                def _():
                    for which in range(3):
                        halo_copy(m, which, d, dr, dc).wait_send()

                @pl.when(inside(dr, dc) & (s == sections - 1))
                def _():
                    out_grad_copy(m, d, dr, dc).wait_send()

            @pl.when((s > 0) & inside(dr, dc))
            def _():
                section_copy(m, d, dr, dc).wait_send()


def on_device(axes, sizes, section_input, first_pre, second_pre, out_grad, kernels, bn_scale, bn_shift):
    sections, rows_n, cols_n = sizes
    micros, rows, cols, width = out_grad.shape
    group = rows_n * cols_n
    tiles = 18 * width // 16
    chunk = 16 * (-(-tiles // group))
    pixels = micros * rows * cols
    factor = 1.0 / (pixels * group) ** 0.5
    parts = 3
    paired = cols_n == 2 and rows_n == 4 and tiles % (4 * parts) == 0
    sub = 16 * tiles // (4 * parts) if paired else 16
    dims = (axes, sections, rows_n, cols_n, factor, paired, chunk)
    pitch = 2 * cols
    dma = pltpu.SemaphoreType.DMA
    field = pltpu.VMEM((micros, rows + 4, pitch, width), BF16)
    peers = max(group - 1, 1)
    wide = micros * rows * pitch if paired else pixels
    hbm = pl.BlockSpec(memory_space=pl.ANY)
    out, grads = pl.pallas_call(
        functools.partial(kernel, dims),
        out_shape=(
            jax.ShapeDtypeStruct(out_grad.shape, BF16),
            jax.ShapeDtypeStruct((group * chunk, width), BF16),
        ),
        in_specs=[hbm] * 7,
        out_specs=(hbm, hbm),
        scratch_shapes=[
            pltpu.VMEM(out_grad.shape, BF16),
            pltpu.VMEM((chunk, width), F32),
            field, field, field, field,
            pltpu.VMEM((2, 9, width, width), BF16),
            pltpu.VMEM((2, width), F32),
            pltpu.VMEM((2, width), F32),
            pltpu.VMEM((2, 9 * width, width), BF16),
            pltpu.VMEM((rows + 2, pitch, width), F32),
            pltpu.VMEM((rows + 4, pitch, width), F32),
            pltpu.VMEM((pixels, 9 * width), BF16),
            pltpu.VMEM((wide, 9 * width), BF16),
            pltpu.VMEM((pixels, width), BF16),
            pltpu.VMEM((micros, rows, pitch, width), BF16),
            pltpu.VMEM((micros, rows + 2, pitch, width), BF16),
            pltpu.VMEM((micros, rows, cols, width), BF16),
            pltpu.VMEM((micros, rows + 2, cols, width), BF16),
            pltpu.VMEM((2 * parts, sub, width), BF16),
            pltpu.VMEM((parts, sub, width), BF16),
            pltpu.VMEM((group * chunk, width), BF16),
            pltpu.VMEM((2 * parts, sub, width) if paired else (peers, chunk, width), BF16),
            pltpu.VMEM((parts, sub, width) if paired else (chunk, width), BF16),
            pltpu.VMEM((parts, sub, width) if paired else (peers, chunk, width), BF16),
            dma((micros + max(group, 4 * parts),)), dma((7,)), dma((micros, 2)), dma((micros, 2)),
            dma((micros, 3, 9)), dma((micros, 3, 9)),
            dma((micros, 9)), dma((micros, 9)), dma((micros, 9)),
            dma((max(peers, 5 * parts),)), dma((max(peers, 5 * parts),)), dma((peers,)), dma((peers,)),
        ],
        compiler_params=pltpu.CompilerParams(
            collective_id=0, has_side_effects=True, vmem_limit_bytes=62 * 1024 * 1024
        ),
    )(
        section_input[0], first_pre[0], second_pre[0], out_grad,
        kernels[0].reshape(2, 9, width, width), bn_scale[0], bn_shift[0],
    )
    grads = grads[: 18 * width].astype(F32).reshape(1, 2, 3, 3, width, width)
    return out[None], grads


def solution(mesh):
    in_specs = (
        P("section", None, "row", "col", None),
        P("section", None, "row", "col", None),
        P("section", None, "row", "col", None),
        P(None, "row", "col", None),
        P("section", None, None, None, None, None),
        P("section", None, None),
        P("section", None, None),
    )
    out_specs = (P("section", None, "row", "col", None), P("section", None, None, None, None, None))
    sizes = tuple(mesh.shape[a] for a in ("section", "row", "col"))
    return jax.shard_map(
        functools.partial(on_device, tuple(mesh.axis_names), sizes),
        mesh=mesh, in_specs=in_specs, out_specs=out_specs, check_vma=False,
    )
```

```python
import functools

import jax
import jax.numpy as jnp
from jax import lax
from jax.experimental import pallas as pl
from jax.experimental.pallas import tpu as pltpu
from jax.sharding import PartitionSpec as P

MESH = pl.DeviceIdType.MESH
SPREAD = [(dr, dc) for dr in (-1, 0, 1) for dc in (-1, 0, 1)]
F32 = jnp.float32
BF16 = jnp.bfloat16


def each(count, body):
    if count <= 16:
        for step in range(count):
            body(step)
    else:

        def run(step, carry):
            body(step)
            return carry

        lax.fori_loop(0, count, run, 0)


def kernel(
    dims, x_ref, p1_ref, p2_ref, og_ref, k_hbm, scale_hbm, shift_hbm,
    out_hbm, fg_hbm,
    out_ref, fg_ref, xf, p1f, p2f, gf, k_ref, scale_ref, shift_ref, kt, c1, c2, cols1, cols2, act,
    union_x, union_g, spare_x, spare_g, crossed, parted, red, inbox, final, gathered,
    stores, local, pair_send, pair_recv, halo_send, halo_recv, og_send, g_send, g_recv, rs_send, rs_recv, ag_send, ag_recv,
):
    axes, sections, rows_n, cols_n, factor, paired, chunk_rows = dims
    micros, rows, cols, width = x_ref.shape
    pitch = 2 * cols
    half = cols // 2
    group = rows_n * cols_n
    chunk = chunk_rows
    s = lax.axis_index("section")
    r = lax.axis_index("row")
    c = lax.axis_index("col")
    me = r * cols_n + c

    def dev(sec, row, col):
        where = {"section": sec, "row": row, "col": col}
        return tuple(where[a] for a in axes)

    def inside(dr, dc):
        return (r + dr >= 0) & (r + dr < rows_n) & (c + dc >= 0) & (c + dc < cols_n)

    def src_part(dr, dc):
        row = {-1: pl.ds(0, 2), 0: pl.ds(0, rows), 1: pl.ds(rows - 2, 2)}[dr]
        col = {-1: pl.ds(0, half), 0: pl.ds(0, cols), 1: pl.ds(half, half)}[dc]
        return row, col

    def dst_part(dr, dc):
        row = {-1: pl.ds(rows + 2, 2), 0: pl.ds(2, rows), 1: pl.ds(0, 2)}[dr]
        col = {-1: pl.ds(cols, half), 0: pl.ds(0, cols), 1: pl.ds(cols + half, half)}[dc]
        return row, col

    def shift_copy(src, dst, m, dr, dc, send, recv, sec):
        a, b = src_part(dr, dc)
        p, q = dst_part(dr, dc)
        if src is dst:
            a = pl.ds(a.start + 2, a.size)
        return pltpu.make_async_remote_copy(
            src_ref=src.at[m, a, b], dst_ref=dst.at[m, p, q],
            send_sem=send, recv_sem=recv,
            device_id=dev(sec, r + dr, c + dc), device_id_type=MESH,
        )

    def centre(ref):
        return ref.at[:, pl.ds(2, rows), pl.ds(0, cols)]

    loads = [
        pltpu.make_async_copy(src, dst, local.at[i])
        for i, (src, dst) in enumerate(
            (
                (p2_ref, centre(p2f)), (x_ref, centre(xf)), (p1_ref, centre(p1f)),
                (scale_hbm, scale_ref), (shift_hbm, shift_ref), (k_hbm, k_ref),
            )
        )
    ]
    og_load = pltpu.make_async_copy(og_ref, centre(gf), local.at[6])

    @pl.when(s == sections - 1)
    def _():
        og_load.start()

    for load in loads:
        load.start()

    for ref in (xf, p1f, p2f, gf):
        for m in range(micros):
            ref[m, 0:2] = jnp.zeros((2, pitch, width), BF16)
            ref[m, rows + 2 : rows + 4] = jnp.zeros((2, pitch, width), BF16)
            ref[m, 2 : rows + 2, cols:pitch] = jnp.zeros((rows, cols, width), BF16)

    barrier = pltpu.get_barrier_semaphore()

    def greet(step):
        peer = lax.rem(me + step + 1, group)
        pl.semaphore_signal(
            barrier, inc=1, device_id=dev(s, peer // cols_n, lax.rem(peer, cols_n)),
            device_id_type=MESH,
        )

    each(group - 1, greet)
    expected = group - 1 + jnp.int32(0)
    for dr, dc in SPREAD:
        expected = expected + jnp.where((s > 0) & inside(dr, dc), 1, 0)

        @pl.when((s < sections - 1) & inside(dr, dc))
        def _():
            pl.semaphore_signal(
                barrier, inc=1, device_id=dev(s + 1, r + dr, c + dc), device_id_type=MESH
            )

    for load in loads[:3]:
        load.wait()

    @pl.when(s == sections - 1)
    def _():
        og_load.wait()

    pl.semaphore_wait(barrier, expected)

    halos = ((p2f, p2f), (xf, xf), (p1f, p1f))
    around = [(d, dr, dc) for d, (dr, dc) in enumerate(SPREAD) if (dr, dc) != (0, 0)]

    def halo_copy(m, which, d, dr, dc):
        src, dst = halos[which]
        return shift_copy(
            src, dst, m, dr, dc, halo_send.at[m, which, d], halo_recv.at[m, which, d], s
        )

    def out_grad_copy(m, d, dr, dc):
        return shift_copy(gf, gf, m, dr, dc, og_send.at[m, d], g_recv.at[m, d], s)

    def section_copy(m, d, dr, dc):
        return shift_copy(
            out_ref, gf, m, dr, dc, g_send.at[m, d], g_recv.at[m, d], s - 1
        )

    for m in range(micros):
        for d, dr, dc in around:

            @pl.when(inside(dr, dc) & (s == sections - 1))
            def _():
                out_grad_copy(m, d, dr, dc).start()

            @pl.when(inside(dr, dc))
            def _():
                for which in range(3):
                    halo_copy(m, which, d, dr, dc).start()

    for load in loads[3:]:
        load.wait()
    for conv in range(2):
        for k in range(9):
            kt[conv, pl.ds(k * width, width), :] = jnp.transpose(k_ref[conv, 8 - k])

    g0 = scale_ref[0:1, :].reshape(1, 1, width)
    g1 = scale_ref[1:2, :].reshape(1, 1, width)
    b0 = shift_ref[0:1, :].reshape(1, 1, width)
    b1 = shift_ref[1:2, :].reshape(1, 1, width)
    own = pl.ds(pl.multiple_of(c * cols, cols), cols)

    def pair_copy(m, which, src, dst):
        return pltpu.make_async_remote_copy(
            src_ref=src.at[m], dst_ref=dst.at[m, :, own],
            send_sem=pair_send.at[m, which], recv_sem=pair_recv.at[m, which],
            device_id=dev(s, r, 1 - c), device_id_type=MESH,
        )

    def pair_arrival(m, which, src, dst):
        other = pl.ds(pl.multiple_of((1 - c) * cols, cols), cols)
        return pltpu.make_async_remote_copy(
            src_ref=src.at[m], dst_ref=dst.at[m, :, other],
            send_sem=pair_send.at[m, which], recv_sem=pair_recv.at[m, which],
            device_id=dev(s, r, 1 - c), device_id_type=MESH,
        )

    pairs = ((spare_x, union_x), (spare_g, union_g))
    for m in range(micros):
        first_norm = g0 * p1f[m, 2 : rows + 2, :cols].astype(F32) + b0
        active = jnp.maximum(first_norm, 0.0)
        if paired:
            inputs = xf[m, 2 : rows + 2, :cols].astype(F32)
            union_x[m, :, own] = jnp.where(c == 0, inputs, active).astype(BF16)
            spare_x[m] = jnp.where(c == 0, active, inputs).astype(BF16)
            pair_copy(m, 0, *pairs[0]).start()
        else:
            act[pl.ds(m * rows * cols, rows * cols), :] = active.astype(BF16).reshape(
                rows * cols, width
            )

    row_i = lax.broadcasted_iota(jnp.int32, (rows + 2, pitch, width), 0)
    col_i = lax.broadcasted_iota(jnp.int32, (rows + 2, pitch, width), 1)
    row_lo = jnp.where(r == 0, 1, 0)
    row_hi = jnp.where(r == rows_n - 1, rows, rows + 1)
    col_hi = jnp.where(c == cols_n - 1, cols, cols + half)
    col_lo = jnp.where(c == 0, pitch, cols + half)
    valid = (
        (row_i >= row_lo) & (row_i <= row_hi) & ((col_i < col_hi) | (col_i >= col_lo))
    )

    def wrapped(field):
        left = pltpu.roll(field, 1, 1)
        right = pltpu.roll(field, pitch - 1, 1)
        return left.astype(BF16), field.astype(BF16), right.astype(BF16)

    def out_store(m):
        return pltpu.make_async_copy(out_ref.at[m], out_hbm.at[m], stores.at[m])

    for m in range(micros):
        for d, dr, dc in around:

            @pl.when(inside(-dr, -dc))
            def _():
                for which in range(3):
                    halo_copy(m, which, d, dr, dc).wait_recv()

        second_norm = g1 * p2f[m].astype(F32) + b1
        c2[...] = jnp.where(second_norm + xf[m].astype(F32) > 0, g1, 0.0)
        first_norm = g0 * p1f[m, pl.ds(1, rows + 2)].astype(F32) + b0
        c1[...] = jnp.where((first_norm > 0) & valid, g0, 0.0)

        for d, (dr, dc) in enumerate(SPREAD):
            if (dr, dc) == (0, 0):

                @pl.when(s < sections - 1)
                def _():
                    section_copy(m, d, dr, dc).wait_recv()
            else:

                @pl.when(inside(-dr, -dc))
                def _():
                    section_copy(m, d, dr, dc).wait_recv()

        incoming = gf[m].astype(F32)
        second_grad = (incoming * c2[...]).astype(BF16).astype(F32)
        acc = None
        moved = wrapped(second_grad)
        base = m * rows * cols
        for i in range(3):
            for j in range(3):
                k = 3 * i + j
                part = moved[j][i : i + rows + 2]
                if not paired:
                    cols2[pl.ds(base, rows * cols), pl.ds(k * width, width)] = part[
                        1 : rows + 1, :cols
                    ].reshape(rows * cols, width)
                term = jnp.dot(
                    part.reshape((rows + 2) * pitch, width),
                    kt[1, pl.ds(k * width, width), :],
                    preferred_element_type=F32,
                )
                acc = term if acc is None else acc + term
        first_grad = (acc.reshape(rows + 2, pitch, width) * c1[...]).astype(BF16).astype(F32)
        if paired:
            second_own = second_grad[1 : rows + 3, :cols]
            first_own = first_grad[:, :cols]
            union_g[m, :, own] = jnp.where(c == 0, first_own, second_own).astype(BF16)
            spare_g[m] = jnp.where(c == 0, second_own, first_own).astype(BF16)
            pair_copy(m, 1, *pairs[1]).start()
        moved = wrapped(first_grad)
        for i in range(3):
            for j in range(3):
                k = 3 * i + j
                cols1[pl.ds(base, rows * cols), pl.ds(k * width, width)] = moved[j][
                    i : i + rows, :cols
                ].reshape(rows * cols, width)
        back = jnp.dot(
            cols1[pl.ds(base, rows * cols), :], kt[0], preferred_element_type=F32
        )
        tile = (pl.ds(2, rows), pl.ds(0, cols))
        masked = jnp.where(c2[tile] > 0, gf[(m, *tile)].astype(F32), 0.0)
        out_ref[m] = (masked + back.reshape(rows, cols, width)).astype(BF16)
        out_store(m).start()
        for d, (dr, dc) in enumerate(SPREAD):

            @pl.when((s > 0) & inside(dr, dc))
            def _():
                section_copy(m, d, dr, dc).start()

    if paired:
        area = rows * pitch
        edge = lax.broadcasted_iota(jnp.int32, (rows + 2, pitch, width), 1)
        for m in range(micros):
            for which in range(2):
                pair_arrival(m, which, *pairs[which]).wait_recv()
            field = union_g[m].astype(F32)
            moved = (
                jnp.where(edge > 0, pltpu.roll(field, 1, 1), 0.0).astype(BF16),
                union_g[m],
                jnp.where(edge < pitch - 1, pltpu.roll(field, pitch - 1, 1), 0.0).astype(BF16),
            )
            for i in range(3):
                for j in range(3):
                    cols2[
                        pl.ds(m * area, area), pl.ds((3 * i + j) * width, width)
                    ] = moved[j][i : i + rows].reshape(area, width)
            term = lax.dot_general(
                union_x[m].reshape(area, width), cols2[pl.ds(m * area, area), :],
                (((0,), (0,)), ((), ())), preferred_element_type=F32,
            )
            total = term if m == 0 else total + term
        for k in range(9):
            red[pl.ds((8 - k) * width, width), :] = (
                total[:, k * width : (k + 1) * width] * factor
            ).astype(BF16)

        parts = parted.shape[0]
        sub = parted.shape[1]
        side = lax.rem(r, 2)
        beside = r + 1 - 2 * side
        across = lax.rem(r + 2, 4)

        def half_rows(which, q):
            return pl.ds(pl.multiple_of((which * parts + q) * sub, 16), sub)

        def send(src, dst, sem, where):
            return pltpu.make_async_remote_copy(
                src_ref=src, dst_ref=dst, send_sem=rs_send.at[sem], recv_sem=rs_recv.at[sem],
                device_id=where, device_id_type=MESH,
            )

        def beside_sum(q):
            return send(red.at[half_rows(1 - side, q)], inbox.at[q], q, dev(s, beside, c))

        def across_sum(q):
            return send(parted.at[q], inbox.at[parts + q], parts + q, dev(s, across, c))

        def beside_copy(q):
            return send(final.at[q], gathered.at[q], 2 * parts + q, dev(s, beside, c))

        def cross_copy(q):
            src = final.at[q] if q < parts else gathered.at[q - parts]
            return send(src, crossed.at[q], 3 * parts + q, dev(s, r, 1 - c))

        def grad_store(src, conv, which, q, slot):
            rows_at = pl.ds(
                pl.multiple_of(((conv * 2 + which) * parts + q) * sub, 16), sub
            )
            return pltpu.make_async_copy(src, fg_hbm.at[rows_at], stores.at[micros + slot])

        written = []
        for q in range(parts):
            beside_sum(q).start()
        for q in range(parts):
            beside_sum(q).wait_recv()
            parted[q] = (
                red[half_rows(side, q), :].astype(F32) + inbox[q].astype(F32)
            ).astype(BF16)
            across_sum(q).start()
        for q in range(parts):
            across_sum(q).wait_recv()
            final[q] = (parted[q].astype(F32) + inbox[parts + q].astype(F32)).astype(BF16)
            beside_copy(q).start()
            cross_copy(q).start()
            written.append(grad_store(final.at[q], c, side, q, q))
            written[-1].start()
        for q in range(parts):
            beside_copy(q).wait_recv()
            cross_copy(parts + q).start()
            written.append(grad_store(gathered.at[q], c, 1 - side, q, parts + q))
            written[-1].start()
        for q in range(2 * parts):
            cross_copy(q).wait_recv()
            which = side if q < parts else 1 - side
            written.append(
                grad_store(crossed.at[q], 1 - c, which, q % parts, 2 * parts + q)
            )
            written[-1].start()
        for q in range(parts):
            beside_sum(q).wait_send()
            across_sum(q).wait_send()
            beside_copy(q).wait_send()
        for q in range(2 * parts):
            cross_copy(q).wait_send()
        for store in written:
            store.wait()
        for m in range(micros):
            for which in range(2):
                pair_copy(m, which, *pairs[which]).wait_send()
    else:
        if red.shape[0] > 18 * width:
            red[pl.ds(18 * width, red.shape[0] - 18 * width), :] = jnp.zeros(
                (red.shape[0] - 18 * width, width), BF16
            )
        pixels = micros * rows * cols
        contract = (((0,), (0,)), ((), ()))
        inputs = xf[:, 2 : rows + 2, :cols].reshape(pixels, width)
        fields = (inputs, act[...])
        for conv, grads in ((1, cols2), (0, cols1)):
            total = lax.dot_general(fields[conv], grads[...], contract, preferred_element_type=F32)
            for k in range(9):
                red[pl.ds((conv * 9 + 8 - k) * width, width), :] = (
                    total[:, k * width : (k + 1) * width] * factor
                ).astype(BF16)

        def piece(index):
            return pl.ds(pl.multiple_of(index * chunk, 16), chunk)

        def peer_of(step):
            peer = lax.rem(me + step + 1, group)
            return peer, dev(s, peer // cols_n, lax.rem(peer, cols_n))

        def rs_copy(step):
            peer, where = peer_of(step)
            return pltpu.make_async_remote_copy(
                src_ref=red.at[piece(peer)], dst_ref=inbox.at[step],
                send_sem=rs_send.at[step], recv_sem=rs_recv.at[step],
                device_id=where, device_id_type=MESH,
            )

        def ag_copy(step):
            peer, where = peer_of(step)
            return pltpu.make_async_remote_copy(
                src_ref=final, dst_ref=gathered.at[step],
                send_sem=ag_send.at[step], recv_sem=ag_recv.at[step],
                device_id=where, device_id_type=MESH,
            )

        each(group - 1, lambda step: rs_copy(step).start())
        fg_ref[...] = red[piece(me), :].astype(F32)

        def gather_in(step):
            rs_copy(step).wait_recv()
            fg_ref[...] += inbox[step].astype(F32)

        each(group - 1, gather_in)
        final[...] = fg_ref[...].astype(BF16)

        def grad_store(src, index, slot):
            return pltpu.make_async_copy(
                src, fg_hbm.at[piece(index)], stores.at[micros + slot]
            )

        grad_store(final, me, group - 1).start()
        each(group - 1, lambda step: ag_copy(step).start())

        def spread_out(step):
            ag_copy(step).wait_recv()
            source = lax.rem(me + group - step - 1, group)
            grad_store(gathered.at[step], source, step).start()

        each(group - 1, spread_out)

        each(group, lambda step: grad_store(final, me, step).wait())
        each(group - 1, lambda step: rs_copy(step).wait_send())
        each(group - 1, lambda step: ag_copy(step).wait_send())
    for m in range(micros):
        out_store(m).wait()
    for m in range(micros):
        for d, (dr, dc) in enumerate(SPREAD):
            if (dr, dc) != (0, 0):

                @pl.when(inside(dr, dc))
                def _():
                    for which in range(3):
                        halo_copy(m, which, d, dr, dc).wait_send()

                @pl.when(inside(dr, dc) & (s == sections - 1))
                def _():
                    out_grad_copy(m, d, dr, dc).wait_send()

            @pl.when((s > 0) & inside(dr, dc))
            def _():
                section_copy(m, d, dr, dc).wait_send()


def on_device(axes, sizes, section_input, first_pre, second_pre, out_grad, kernels, bn_scale, bn_shift):
    sections, rows_n, cols_n = sizes
    micros, rows, cols, width = out_grad.shape
    group = rows_n * cols_n
    tiles = 18 * width // 16
    chunk = 16 * (-(-tiles // group))
    pixels = micros * rows * cols
    factor = 1.0 / (pixels * group) ** 0.5
    parts = 3
    paired = cols_n == 2 and rows_n == 4 and tiles % (4 * parts) == 0
    sub = 16 * tiles // (4 * parts) if paired else 16
    dims = (axes, sections, rows_n, cols_n, factor, paired, chunk)
    pitch = 2 * cols
    dma = pltpu.SemaphoreType.DMA
    field = pltpu.VMEM((micros, rows + 4, pitch, width), BF16)
    peers = max(group - 1, 1)
    wide = micros * rows * pitch if paired else pixels
    hbm = pl.BlockSpec(memory_space=pl.ANY)
    out, grads = pl.pallas_call(
        functools.partial(kernel, dims),
        out_shape=(
            jax.ShapeDtypeStruct(out_grad.shape, BF16),
            jax.ShapeDtypeStruct((group * chunk, width), BF16),
        ),
        in_specs=[hbm] * 7,
        out_specs=(hbm, hbm),
        scratch_shapes=[
            pltpu.VMEM(out_grad.shape, BF16),
            pltpu.VMEM((chunk, width), F32),
            field, field, field, field,
            pltpu.VMEM((2, 9, width, width), BF16),
            pltpu.VMEM((2, width), F32),
            pltpu.VMEM((2, width), F32),
            pltpu.VMEM((2, 9 * width, width), BF16),
            pltpu.VMEM((rows + 2, pitch, width), F32),
            pltpu.VMEM((rows + 4, pitch, width), F32),
            pltpu.VMEM((pixels, 9 * width), BF16),
            pltpu.VMEM((wide, 9 * width), BF16),
            pltpu.VMEM((pixels, width), BF16),
            pltpu.VMEM((micros, rows, pitch, width), BF16),
            pltpu.VMEM((micros, rows + 2, pitch, width), BF16),
            pltpu.VMEM((micros, rows, cols, width), BF16),
            pltpu.VMEM((micros, rows + 2, cols, width), BF16),
            pltpu.VMEM((2 * parts, sub, width), BF16),
            pltpu.VMEM((parts, sub, width), BF16),
            pltpu.VMEM((group * chunk, width), BF16),
            pltpu.VMEM((2 * parts, sub, width) if paired else (peers, chunk, width), BF16),
            pltpu.VMEM((parts, sub, width) if paired else (chunk, width), BF16),
            pltpu.VMEM((parts, sub, width) if paired else (peers, chunk, width), BF16),
            dma((micros + max(group, 4 * parts),)), dma((7,)), dma((micros, 2)), dma((micros, 2)),
            dma((micros, 3, 9)), dma((micros, 3, 9)),
            dma((micros, 9)), dma((micros, 9)), dma((micros, 9)),
            dma((max(peers, 5 * parts),)), dma((max(peers, 5 * parts),)), dma((peers,)), dma((peers,)),
        ],
        compiler_params=pltpu.CompilerParams(
            collective_id=0, has_side_effects=True, vmem_limit_bytes=62 * 1024 * 1024
        ),
    )(
        section_input[0], first_pre[0], second_pre[0], out_grad,
        kernels[0].reshape(2, 9, width, width), bn_scale[0], bn_shift[0],
    )
    grads = grads[: 18 * width].astype(F32).reshape(1, 2, 3, 3, width, width)
    return out[None], grads


def solution(mesh):
    in_specs = (
        P("section", None, "row", "col", None),
        P("section", None, "row", "col", None),
        P("section", None, "row", "col", None),
        P(None, "row", "col", None),
        P("section", None, None, None, None, None),
        P("section", None, None),
        P("section", None, None),
    )
    out_specs = (P("section", None, "row", "col", None), P("section", None, None, None, None, None))
    sizes = tuple(mesh.shape[a] for a in ("section", "row", "col"))
    return jax.shard_map(
        functools.partial(on_device, tuple(mesh.axis_names), sizes),
        mesh=mesh, in_specs=in_specs, out_specs=out_specs, check_vma=False,
    )
```
